128 devices in a mesh: ctx: 16 (over x_hi, z, core), head: 8 (over y, x_lo).
Axes of the slice: x: 4 (x_hi: 2, x_lo: 2; x = x_hi * 2 + x_lo), y: 4, z: 4, core: 2. Of those that a mesh axis runs over, the one named last changes fastest.
Arguments:
- queries: bfloat16 [16384, 32, 128], P('ctx', 'head'), may hold values from -64 to 64
- keys: bfloat16 [16384, 8, 128], P('ctx', 'head'), may hold values from -5 to 5
- values: bfloat16 [16384, 8, 128], P('ctx', 'head'), may hold values from -6 to 6
- grad_out: bfloat16 [16384, 32, 128], P('ctx', 'head'), may hold values from -6 to 6
- doc_lengths: int32 [8], replicated, may hold values from 1 to 4096, 16384 in all
- block_plan: int32 [32], replicated, may hold values from 0 to 31, each once
Outputs:
- attn_out: bfloat16 [16384, 32, 128], P('ctx', 'head')
- grad_queries: bfloat16 [16384, 32, 128], P('ctx', 'head')
- grad_keys: bfloat16 [16384, 8, 128], P('ctx', 'head')
- grad_values: bfloat16 [16384, 8, 128], P('ctx', 'head')
The draws below stay inside these ranges and needn't reach their ends.
Inputs may be any that keep to these rules, and one draw needn't show every extreme that they name: `block_plan`: a permutation of the 32 position blocks. `doc_lengths`: they sum to 16384; some document has exactly 4096 tokens.
All inputs are finite; a program needn't handle non-finite values.
Results may differ from the reference program's by a relative error of at most 0.025.
Values may be sent and summed in bfloat16 or wider, within the bound.
A program may use at most 128 MiB of HBM per device.

```python
import math
import jax
import jax.numpy as jnp
import numpy as np
from jax import lax

DH = 128
GROUP = 4
BLK = 512
KVH = 8
QH = 32
TOKENS = 16384
NBLK = 32
DOC_MOST = 4096
NDOC = 8


def shared_keys(key):
    base = jnp.clip(jax.random.normal(jax.random.fold_in(key, 11), (TOKENS, KVH, DH), jnp.float32), -5.0, 5.0)
    return base


def draw_keys(key, part):
    base = shared_keys(key)
    return base.astype(jnp.bfloat16)


def draw_queries(key, part):
    drawn = jnp.clip(jax.random.normal(jax.random.fold_in(key, 13), (TOKENS, QH, DH), jnp.float32), -6.0, 6.0)
    return drawn.astype(jnp.bfloat16)


def block_levels(stream_key, shape, split, smallest, largest):
    def one(position, shards_of):
        steps = jax.random.uniform(jax.random.fold_in(jax.random.fold_in(stream_key, 6), position), (shards_of,), jnp.float32, smallest / len(split), largest / len(split))
        return jnp.repeat(jnp.exp(steps), shape[position] // shards_of).reshape((-1,) + (1,) * (len(shape) - position - 1))

    gain = one(*split[0])
    for cut in split[1:]:
        gain = gain * one(*cut)
    return gain


def length_profile(count, total, most, lean):
    weights = [(1 << 20) // math.isqrt(grade ** lean) + 1 for grade in range(2, count + 1)]
    rest, given = total - most - (count - 1), [1] * (count - 1)
    while rest > 0:
        movable = [i for i in range(count - 1) if given[i] < most]
        mass, budget = sum([weights[i] for i in movable]), rest
        for i in movable:
            addition = min(most - given[i], max(1, budget * weights[i] // mass), rest)
            given[i] = given[i] + addition
            rest = rest - addition
    return np.array([most] + given)


def uneven_parts(own_key, count, total, bound, slope):
    if count == 2:
        one = jax.random.randint(own_key, (), max(1, total - bound), min(bound, total - 1) + 1)
        return jnp.stack([one, total - one])
    lengths = jnp.asarray(length_profile(count, total, bound, slope), jnp.int32)
    couples = (count - 1) // 2
    giver, receiver = lengths[1:1 + 2 * couples:2], lengths[2:2 + 2 * couples:2]
    slack = jnp.minimum(giver - 1, bound - receiver)
    passed = jax.random.randint(jax.random.fold_in(own_key, 1), (couples,), 0, 1 << 20) % (slack + 1)
    lengths = lengths.at[1:1 + 2 * couples:2].set(giver - passed).at[2:2 + 2 * couples:2].set(receiver + passed)
    return lengths[jax.random.permutation(jax.random.fold_in(own_key, 2), count)]


def scatter_about(rng, dims, scale, bound, split=(), kind=jnp.bfloat16):
    loudness = block_levels(rng, dims, split, -0.22, 0.18) if split else 1.0
    drawn = jax.random.normal(rng, dims, jnp.float32) * scale * loudness
    return jnp.minimum(jnp.maximum(drawn, -bound), bound).astype(kind)


def setup_inputs(seed: int = 0) -> dict:
    streams_of = jax.random.split(jax.random.key(seed), 7)
    queries = draw_queries(jax.random.fold_in(streams_of[6], 71), 0)
    keys = draw_keys(jax.random.fold_in(streams_of[6], 71), 0)
    values = scatter_about(streams_of[2], (TOKENS, KVH, DH), 1.0, 6.0, ((0, 16), (1, 8)))
    grad_out = scatter_about(streams_of[3], (TOKENS, QH, DH), 1.0, 6.0, ((0, 16), (1, 8)))
    doc_lengths = uneven_parts(streams_of[4], NDOC, TOKENS, DOC_MOST, 2).astype(jnp.int32)
    block_plan = jax.random.permutation(streams_of[5], NBLK).astype(jnp.int32)
    return {"queries": queries, "keys": keys, "values": values, "grad_out": grad_out, "doc_lengths": doc_lengths, "block_plan": block_plan}


NEG = -1e+30

def reference(queries, keys, values, grad_out, doc_lengths, block_plan):
    total = queries.shape[0]
    n_blocks = total // BLK
    width = DOC_MOST + BLK
    scale = 1.0 / math.sqrt(DH)
    offsets = jnp.arange(BLK, dtype=jnp.int32)
    plan = block_plan.astype(jnp.int32)
    row_pos = (plan[:, None] * BLK + offsets[None, :]).reshape(total)
    inverse = jnp.zeros((n_blocks,), jnp.int32).at[plan].set(jnp.arange(n_blocks, dtype=jnp.int32))
    pos_row = (inverse[:, None] * BLK + offsets[None, :]).reshape(total)
    ends = jnp.cumsum(doc_lengths.astype(jnp.int32))
    positions = jnp.arange(total, dtype=jnp.int32)
    doc_of = lax.optimization_barrier(jnp.sum((positions[:, None] >= ends[None, :]).astype(jnp.int32), axis=1))
    q_ord = queries[pos_row]
    g_ord = grad_out[pos_row]
    k_pad = jnp.concatenate([jnp.zeros((DOC_MOST, KVH, DH), keys.dtype), keys[pos_row]], axis=0)
    v_pad = jnp.concatenate([jnp.zeros((DOC_MOST, KVH, DH), values.dtype), values[pos_row]], axis=0)
    doc_pad = jnp.concatenate([jnp.full((DOC_MOST,), -1, jnp.int32), doc_of])
    pos_pad = jnp.concatenate([jnp.full((DOC_MOST,), -1, jnp.int32), positions])

    def per_head(group):
        q_head = lax.dynamic_slice_in_dim(q_ord, group * GROUP, GROUP, 1)
        g_head = lax.dynamic_slice_in_dim(g_ord, group * GROUP, GROUP, 1)
        k_head = lax.dynamic_index_in_dim(k_pad, group, 1, keepdims=False)
        v_head = lax.dynamic_index_in_dim(v_pad, group, 1, keepdims=False)

        def step(carry, block):
            dk_acc, dv_acc = carry
            start = block * BLK
            qb = lax.dynamic_slice_in_dim(q_head, start, BLK, 0).astype(jnp.float32)
            gb = lax.dynamic_slice_in_dim(g_head, start, BLK, 0).astype(jnp.float32)
            kw = lax.dynamic_slice_in_dim(k_head, start, width, 0).astype(jnp.float32)
            vw = lax.dynamic_slice_in_dim(v_head, start, width, 0).astype(jnp.float32)
            q_doc = lax.dynamic_slice_in_dim(doc_of, start, BLK, 0)
            q_pos = start + offsets
            k_doc = lax.dynamic_slice_in_dim(doc_pad, start, width, 0)
            k_pos = lax.dynamic_slice_in_dim(pos_pad, start, width, 0)
            mask = (k_doc[None, :] == q_doc[:, None]) & (k_pos[None, :] <= q_pos[:, None])
            scores = jnp.einsum('qgd,kd->gqk', qb, kw) * scale
            masked = jnp.where(mask[None], scores, NEG)
            top = lax.optimization_barrier(jnp.max(masked, axis=-1))
            lse = top + jnp.log(lax.optimization_barrier(jnp.sum(jnp.where(mask[None], jnp.exp(masked - top[..., None]), 0.0), axis=-1)))
            probs = jnp.where(mask[None], jnp.exp(scores - lse[..., None]), 0.0)
            weights = lax.optimization_barrier(probs.astype(jnp.bfloat16)).astype(jnp.float32)
            out = jnp.einsum('gqk,kd->gqd', weights, vw).astype(jnp.bfloat16)
            delta = lax.optimization_barrier(jnp.sum(out.astype(jnp.float32) * jnp.transpose(gb, (1, 0, 2)), axis=-1))
            dprob = jnp.einsum('qgd,kd->gqk', gb, vw)
            dscore = lax.optimization_barrier((probs * (dprob - delta[..., None])).astype(jnp.bfloat16)).astype(jnp.float32)
            dq_blk = (jnp.einsum('gqk,kd->gqd', dscore, kw) * scale).astype(jnp.bfloat16)
            dk_win = jnp.einsum('gqk,qgd->kd', dscore, qb) * scale
            dv_win = jnp.einsum('gqk,qgd->kd', weights, gb)
            dk_acc = lax.dynamic_update_slice_in_dim(dk_acc, lax.dynamic_slice_in_dim(dk_acc, start, width, 0) + dk_win, start, 0)
            dv_acc = lax.dynamic_update_slice_in_dim(dv_acc, lax.dynamic_slice_in_dim(dv_acc, start, width, 0) + dv_win, start, 0)
            return ((dk_acc, dv_acc), (out, dq_blk))
        zero = jnp.zeros((total + DOC_MOST, DH), jnp.float32)
        (dk_acc, dv_acc), (outs, dqs) = lax.scan(step, (zero, zero), jnp.arange(n_blocks, dtype=jnp.int32))
        return (outs, dqs, dk_acc[DOC_MOST:], dv_acc[DOC_MOST:])
    outs, dqs, dks, dvs = lax.map(per_head, jnp.arange(KVH, dtype=jnp.int32))
    out_pos = jnp.transpose(outs, (1, 3, 0, 2, 4)).reshape(total, QH, DH)
    dq_pos = jnp.transpose(dqs, (1, 3, 0, 2, 4)).reshape(total, QH, DH)
    dk_pos = jnp.transpose(dks, (1, 0, 2))
    dv_pos = jnp.transpose(dvs, (1, 0, 2))
    attn_out = out_pos[row_pos]
    grad_queries = dq_pos[row_pos]
    grad_keys = dk_pos[row_pos].astype(jnp.bfloat16)
    grad_values = dv_pos[row_pos].astype(jnp.bfloat16)
    return (attn_out, grad_queries, grad_keys, grad_values)
```

```python
import math

import jax
import jax.numpy as jnp
from jax import lax
from jax.experimental import pallas as pl
from jax.experimental.pallas import tpu as pltpu
from jax.sharding import PartitionSpec as P

DH = 128
GROUP = 4
BLK = 512
DOC_MOST = 4096
NDOC = 8
QT = 256
ROWS = QT * GROUP
KT = 256
MAXT = (DOC_MOST + QT) // KT
CH = 256
PER = 1024
NEG = -1e30
SCALE = 1.0 / math.sqrt(DH)
CONST = SCALE * math.log2(math.e)
F32 = jnp.float32
BF16 = jnp.bfloat16


def mm(a, b):
    return jnp.dot(a, b, preferred_element_type=F32)


def attend_kernel(
    rank_ref, len_ref, plan_ref, q_ref, g_ref, kv_ref, o_ref, dq_ref, dkv_ref,
    inv_ref, end_ref, s_ref, p_ref, dkv_acc, qt_ref, gt_ref, gs_ref, m_ref, acc_ref, dqt_ref, stage, sem,
):
    n_blocks = plan_ref.shape[0]
    n_own = kv_ref.shape[0] // (2 * PER)
    rank = rank_ref[0]

    def invert(i, c):
        inv_ref[plan_ref[i]] = i
        return c

    lax.fori_loop(0, n_blocks, invert, 0)
    end_ref[0] = 0
    for d in range(NDOC):
        end_ref[d + 1] = end_ref[d] + len_ref[d]

    def zero(i, c):
        dkv_acc[pl.ds(pl.multiple_of(i * 256, 256), 256), :] = jnp.zeros((256, DH), F32)
        return c

    lax.fori_loop(0, dkv_acc.shape[0] // 256, zero, 0)

    def start_of(position):
        first = jnp.int32(0)
        for d in range(1, NDOC):
            first = jnp.where(position >= end_ref[d], end_ref[d], first)
        return first

    def key_base(kt):
        rb = inv_ref[kt // 2]
        return pl.multiple_of((rb // 2) * (2 * PER) + (rb % 2) * BLK + (kt % 2) * KT, KT)

    def tile(u, c):
        block = u // 2
        pos0 = plan_ref[rank * 2 + block] * BLK + (u % 2) * QT
        rows = pl.ds(pl.multiple_of(u * ROWS, ROWS), ROWS)
        last = pos0 // KT
        first = start_of(pos0) // KT
        full_from = start_of(pos0 + QT - 1)
        count = last - first + 1
        q_pos = pos0 + lax.broadcasted_iota(jnp.int32, (1, ROWS), 1) // GROUP
        q_lo = jnp.zeros((1, ROWS), jnp.int32)
        for d in range(1, NDOC):
            q_lo = jnp.where(q_pos >= end_ref[d], end_ref[d], q_lo)
        qt_ref[...] = q_ref[rows, :].T
        m_ref[...] = jnp.full(m_ref.shape, NEG, F32)
        acc_ref[...] = jnp.zeros(acc_ref.shape, F32)
        dqt_ref[...] = jnp.zeros(dqt_ref.shape, F32)

        def scores(t, c):
            kt = first + t
            k = kv_ref[pl.ds(key_base(kt), KT), :]
            out_rows = pl.ds(pl.multiple_of(t * KT, KT), KT)
            whole = (kt < last) & (kt * KT >= full_from)

            @pl.when(whole)
            def _():
                for c0 in range(0, ROWS, CH):
                    s = mm(k, qt_ref[:, c0 : c0 + CH]) * CONST
                    s_ref[out_rows, c0 : c0 + CH] = s
                    m_ref[:, c0 : c0 + CH] = jnp.maximum(
                        m_ref[:, c0 : c0 + CH], jnp.max(s.reshape(KT // 8, 8, CH), axis=0)
                    )

            @pl.when(jnp.logical_not(whole))
            def _():
                k_pos = kt * KT + lax.broadcasted_iota(jnp.int32, (KT, 1), 0)
                for c0 in range(0, ROWS, CH):
                    s = mm(k, qt_ref[:, c0 : c0 + CH]) * CONST
                    seen = (k_pos >= q_lo[:, c0 : c0 + CH]) & (k_pos <= q_pos[:, c0 : c0 + CH])
                    s = jnp.where(seen, s, NEG)
                    s_ref[out_rows, c0 : c0 + CH] = s
                    m_ref[:, c0 : c0 + CH] = jnp.maximum(
                        m_ref[:, c0 : c0 + CH], jnp.max(s.reshape(KT // 8, 8, CH), axis=0)
                    )

            return c

        lax.fori_loop(0, count, scores, 0)
        top = jnp.max(m_ref[...], axis=0, keepdims=True)
        m_ref[0:1, :] = top

        def outputs(t, c):
            v = kv_ref[pl.ds(key_base(first + t) + PER, KT), :]
            vt = jnp.concatenate([v.T, jnp.ones((16, KT), BF16)], axis=0)
            out_rows = pl.ds(pl.multiple_of(t * KT, KT), KT)
            for c0 in range(0, ROWS, CH):
                p = jnp.exp2(s_ref[out_rows, c0 : c0 + CH] - m_ref[0:1, c0 : c0 + CH]).astype(BF16)
                p_ref[out_rows, c0 : c0 + CH] = p
                acc_ref[:, c0 : c0 + CH] += mm(vt, p)
            return c

        lax.fori_loop(0, count, outputs, 0)
        inv_sum = 1.0 / acc_ref[DH : DH + 1, :]
        out_t = (acc_ref[0:DH, :] * inv_sum).astype(BF16)
        o_ref[rows, :] = out_t.T
        g_t = (g_ref[rows, :].T.astype(F32) * inv_sum).astype(BF16)
        gt_ref[...] = g_t
        gs_ref[...] = g_t.T
        m_ref[1:2, :] = jnp.sum(out_t.astype(F32) * g_t.astype(F32), axis=0, keepdims=True)

        def grads(t, c):
            base = key_base(first + t)
            k = kv_ref[pl.ds(base, KT), :]
            v = kv_ref[pl.ds(base + PER, KT), :]
            kt_ = k.T
            in_rows = pl.ds(pl.multiple_of(t * KT, KT), KT)
            dk = dkv_acc[pl.ds(base, KT), :]
            dv = dkv_acc[pl.ds(base + PER, KT), :]
            for c0 in range(0, ROWS, CH):
                cols = pl.ds(c0, CH)
                p = p_ref[in_rows, cols]
                dv = dv + mm(p, gs_ref[cols, :])
                dp = mm(v, gt_ref[:, cols])
                ds = (p.astype(F32) * (dp - m_ref[1:2, cols])).astype(BF16)
                dk = dk + mm(ds, q_ref[pl.ds(u * ROWS + c0, CH), :])
                dqt_ref[:, cols] += mm(kt_, ds)
            dkv_acc[pl.ds(base, KT), :] = dk
            dkv_acc[pl.ds(base + PER, KT), :] = dv
            return c

        lax.fori_loop(0, count, grads, 0)
        dq_ref[rows, :] = (dqt_ref[...] * SCALE).astype(BF16).T
        return c

    lax.fori_loop(0, q_ref.shape[0] // ROWS, tile, 0)

    def write(i):
        return pltpu.make_async_copy(
            stage.at[i % 2], dkv_ref.at[pl.ds(pl.multiple_of(i * PER, PER), PER), :], sem.at[i % 2]
        )

    def flush(i, c):
        @pl.when(i >= 2)
        def _():
            write(i - 2).wait()

        factor = jnp.where(i % 2 == 0, SCALE, 1.0)
        slot = i % 2
        for r in range(0, PER, 256):
            part = dkv_acc[pl.ds(pl.multiple_of(i * PER + r, 256), 256), :]
            stage[slot, r : r + 256, :] = (part * factor).astype(BF16)
        write(i).start()
        return c

    lax.fori_loop(0, 2 * n_own, flush, 0)
    write(2 * n_own - 2).wait()
    write(2 * n_own - 1).wait()


def attend(rank, doc_lengths, block_plan, q, g, kv):
    n_rows = q.shape[0]
    n_kv = kv.shape[0]
    smem = pl.BlockSpec(memory_space=pltpu.SMEM)
    vmem = pl.BlockSpec(memory_space=pltpu.VMEM)
    return pl.pallas_call(
        attend_kernel,
        out_shape=(
            jax.ShapeDtypeStruct((n_rows, DH), BF16),
            jax.ShapeDtypeStruct((n_rows, DH), BF16),
            jax.ShapeDtypeStruct((n_kv, DH), BF16),
        ),
        in_specs=[smem, smem, smem, vmem, vmem, vmem],
        out_specs=(vmem, vmem, pl.BlockSpec(memory_space=pl.ANY)),
        scratch_shapes=[
            pltpu.SMEM((block_plan.shape[0],), jnp.int32),
            pltpu.SMEM((NDOC + 1,), jnp.int32),
            pltpu.VMEM((MAXT * KT, ROWS), F32),
            pltpu.VMEM((MAXT * KT, ROWS), BF16),
            pltpu.VMEM((n_kv, DH), F32),
            pltpu.VMEM((DH, ROWS), BF16),
            pltpu.VMEM((DH, ROWS), BF16),
            pltpu.VMEM((ROWS, DH), BF16),
            pltpu.VMEM((8, ROWS), F32),
            pltpu.VMEM((DH + 16, ROWS), F32),
            pltpu.VMEM((DH, ROWS), F32),
            pltpu.VMEM((2, PER, DH), BF16),
            pltpu.SemaphoreType.DMA((2,)),
        ],
        compiler_params=pltpu.CompilerParams(vmem_limit_bytes=67043328),
    )(rank, doc_lengths, block_plan, q, g, kv)


MESH = pl.DeviceIdType.MESH
NZ = 4


def place():
    me = lax.axis_index("ctx")
    core = me % 2
    z = (me // 2) % NZ
    x = me // (2 * NZ)

    def at(dx, dz, dc):
        return (((x + dx) % 2) * NZ + (z + dz) % NZ) * 2 + (core + dc) % 2

    return at


def meet(peers):
    barrier = pltpu.get_barrier_semaphore()
    for peer in peers:
        pl.semaphore_signal(barrier, inc=1, device_id={"ctx": peer}, device_id_type=MESH)
    pl.semaphore_wait(barrier, len(peers))


def gather_kernel(k_ref, v_ref, out_ref, own_sem, send_sem, recv_sem):
    at = place()
    me, other, up, down, twin = at(0, 0, 0), at(1, 0, 0), at(0, 1, 0), at(0, NZ - 1, 0), at(0, 0, 1)
    meet((other, up, down, twin))

    def slot(owner, j):
        return out_ref.at[pl.ds(pl.multiple_of((owner * 2 + j) * PER, PER), PER), :]

    sent = []

    def send(owner, j, target, source=None):
        copy = pltpu.make_async_remote_copy(
            src_ref=slot(owner, j) if source is None else source,
            dst_ref=slot(owner, j),
            send_sem=send_sem.at[len(sent)],
            recv_sem=recv_sem.at[owner * 2 + j],
            device_id={"ctx": target},
            device_id_type=MESH,
        )
        copy.start()
        sent.append(copy)

    def arrive(owner, j):
        pltpu.make_async_copy(slot(owner, j), slot(owner, j), recv_sem.at[owner * 2 + j]).wait()

    mine = (k_ref, v_ref)
    for j in (0, 1):
        for target in (other, up, down, twin):
            send(me, j, target, mine[j])
    keep = [pltpu.make_async_copy(mine[j], slot(me, j), own_sem.at[j]) for j in (0, 1)]
    for copy in keep:
        copy.start()

    def relay(dx, dz, j, targets):
        owner = at(dx, dz, 0)
        arrive(owner, j)
        for target in targets:
            send(owner, j, target)

    relay(0, NZ - 1, 0, (up, twin))
    relay(0, 1, 0, (twin,))
    relay(1, 0, 0, (up, down, twin))
    relay(0, 1, 1, (down, twin))
    relay(0, NZ - 1, 1, (twin,))
    relay(1, 0, 1, (up, down, twin))
    relay(0, 2, 0, (twin,))
    relay(0, 2, 1, (twin,))
    relay(1, NZ - 1, 0, (up, twin))
    relay(1, 1, 0, (twin,))
    relay(1, 1, 1, (down, twin))
    relay(1, NZ - 1, 1, (twin,))
    relay(1, 2, 0, (twin,))
    relay(1, 2, 1, (twin,))
    for dx in (0, 1):
        for dz in range(NZ):
            for j in (0, 1):
                arrive(at(dx, dz, 1), j)
    for copy in keep:
        copy.wait()
    for copy in sent:
        copy.wait_send()


def gather(k, v, n_ctx):
    vmem = pl.BlockSpec(memory_space=pltpu.VMEM)
    return pl.pallas_call(
        gather_kernel,
        out_shape=jax.ShapeDtypeStruct((n_ctx * 2 * PER, DH), BF16),
        in_specs=[vmem, vmem],
        out_specs=pl.BlockSpec(memory_space=pl.ANY),
        scratch_shapes=[
            pltpu.SemaphoreType.DMA((2,)),
            pltpu.SemaphoreType.DMA((30,)),
            pltpu.SemaphoreType.DMA((2 * n_ctx,)),
        ],
        compiler_params=pltpu.CompilerParams(collective_id=1, has_side_effects=True),
    )(k, v)


def reduce_kernel(
    part_ref, dk_ref, dv_ref, mine, sib, rel, zin, xin, load_sem, send_sem, sib_sem, rel_sem, zin_sem, xin_sem
):
    at = place()
    other, up, down, twin = at(1, 0, 0), at(0, 1, 0), at(0, NZ - 1, 0), at(0, 0, 1)
    meet((other, up, down, twin))
    sent = []

    def send(source, target_ref, sem, target):
        copy = pltpu.make_async_remote_copy(
            src_ref=source,
            dst_ref=target_ref,
            send_sem=send_sem.at[len(sent)],
            recv_sem=sem,
            device_id={"ctx": target},
            device_id_type=MESH,
        )
        copy.start()
        sent.append(copy)

    def arrive(ref, sem):
        pltpu.make_async_copy(ref, ref, sem).wait()

    def rows_of(owner):
        return part_ref.at[pl.ds(pl.multiple_of(owner * 2 * PER, 2 * PER), 2 * PER), :]

    order = [(1, 2), (0, 2), (1, 1), (1, NZ - 1), (0, 1), (0, NZ - 1), (1, 0), (0, 0)]
    loads = {}
    for n, (dx, dz) in enumerate(order):
        send(rows_of(at(dx, dz, 1)), sib.at[n], sib_sem.at[n], twin)
        loads[n] = pltpu.make_async_copy(rows_of(at(dx, dz, 0)), mine.at[n], load_sem.at[n])
        loads[n].start()
    index = {key: n for n, key in enumerate(order)}

    def add(target, others, count=PER):
        step = 256

        def body(i, c):
            rows = pl.ds(pl.multiple_of(i * step, step), step)
            total = target[rows, :].astype(F32)
            for ref in others:
                total = total + ref[rows, :].astype(F32)
            target[rows, :] = total.astype(BF16)
            return c

        lax.fori_loop(0, count // step, body, 0)

    def pair(dx, dz):
        n = index[(dx, dz)]
        loads[n].wait()
        arrive(sib.at[n], sib_sem.at[n])
        add(mine.at[n], [sib.at[n]], 2 * PER)
        return mine.at[n]

    def half(ref, j):
        return ref.at[pl.ds(j * PER, PER), :]

    for dx in (1, 0):
        total = pair(dx, 2)
        send(half(total, 0), rel.at[dx, 0], rel_sem.at[dx, 0], up)
        send(half(total, 1), rel.at[dx, 1], rel_sem.at[dx, 1], down)
    for dx in (1, 0):
        above = pair(dx, 1)
        send(half(above, 1), half(zin.at[dx, 0], 1), zin_sem.at[dx, 0, 1], up)
        below = pair(dx, NZ - 1)
        send(half(below, 0), half(zin.at[dx, 1], 0), zin_sem.at[dx, 1, 0], down)
        arrive(rel.at[dx, 0], rel_sem.at[dx, 0])
        add(half(above, 0), [rel.at[dx, 0]])
        send(half(above, 0), half(zin.at[dx, 0], 0), zin_sem.at[dx, 0, 0], up)
        arrive(rel.at[dx, 1], rel_sem.at[dx, 1])
        add(half(below, 1), [rel.at[dx, 1]])
        send(half(below, 1), half(zin.at[dx, 1], 1), zin_sem.at[dx, 1, 1], down)
    outs = (dk_ref, dv_ref)
    far = pair(1, 0)
    near = pair(0, 0)
    for j in (1, 0):
        for side in (0, 1):
            arrive(half(zin.at[1, side], j), zin_sem.at[1, side, j])
        add(half(far, j), [half(zin.at[1, 0], j), half(zin.at[1, 1], j)])
        send(half(far, j), half(xin, j), xin_sem.at[j], other)
    for j in (1, 0):
        for side in (0, 1):
            arrive(half(zin.at[0, side], j), zin_sem.at[0, side, j])
    for j in (1, 0):
        arrive(half(xin, j), xin_sem.at[j])

        def body(i, c, j=j):
            rows = pl.ds(pl.multiple_of(i * 256, 256), 256)
            total = half(near, j)[rows, :].astype(F32)
            for ref in (half(zin.at[0, 0], j), half(zin.at[0, 1], j), half(xin, j)):
                total = total + ref[rows, :].astype(F32)
            outs[j][rows, :] = total.astype(BF16)
            return c

        lax.fori_loop(0, PER // 256, body, 0)
    for copy in sent:
        copy.wait_send()


def reduce(part):
    vmem = pl.BlockSpec(memory_space=pltpu.VMEM)
    dma = pltpu.SemaphoreType.DMA
    return pl.pallas_call(
        reduce_kernel,
        out_shape=(jax.ShapeDtypeStruct((PER, DH), BF16),) * 2,
        in_specs=[pl.BlockSpec(memory_space=pl.ANY)],
        out_specs=(vmem, vmem),
        scratch_shapes=[
            pltpu.VMEM((8, 2 * PER, DH), BF16),
            pltpu.VMEM((8, 2 * PER, DH), BF16),
            pltpu.VMEM((2, 2, PER, DH), BF16),
            pltpu.VMEM((2, 2, 2 * PER, DH), BF16),
            pltpu.VMEM((2 * PER, DH), BF16),
            dma((8,)),
            dma((22,)),
            dma((8,)),
            dma((2, 2)),
            dma((2, 2, 2)),
            dma((2,)),
        ],
        compiler_params=pltpu.CompilerParams(
            collective_id=2, has_side_effects=True, vmem_limit_bytes=67043328
        ),
    )(part)


def shards(queries, keys, values, grad_out, doc_lengths, block_plan):
    tok = queries.shape[0]
    n_ctx = lax.axis_size("ctx")
    rank = lax.axis_index("ctx").astype(jnp.int32).reshape(1)
    kv = gather(keys.reshape(tok, DH), values.reshape(tok, DH), n_ctx)
    out, dq, part = attend(
        rank,
        doc_lengths,
        block_plan,
        queries.reshape(tok * GROUP, DH),
        grad_out.reshape(tok * GROUP, DH),
        kv,
    )
    dk, dv = reduce(part)
    return (
        out.reshape(tok, GROUP, DH),
        dq.reshape(tok, GROUP, DH),
        dk.reshape(tok, 1, DH),
        dv.reshape(tok, 1, DH),
    )


def solution(mesh):
    split = P("ctx", "head", None)
    return jax.shard_map(
        shards,
        mesh=mesh,
        in_specs=(split, split, split, split, P(), P()),
        out_specs=(split, split, split, split),
        check_vma=False,
    )
```

```python
import math

import jax
import jax.numpy as jnp
from jax import lax
from jax.experimental import pallas as pl
from jax.experimental.pallas import tpu as pltpu
from jax.sharding import PartitionSpec as P

DH = 128
GROUP = 4
BLK = 512
DOC_MOST = 4096
NDOC = 8
QT = 256
ROWS = QT * GROUP
KT = 256
UNROLL = 2
MAXT = (DOC_MOST + QT) // KT
TILES = 4
PER = 1024
NEG = -1e30
SCALE = 1.0 / math.sqrt(DH)
CONST = SCALE * math.log2(math.e)
F32 = jnp.float32
BF16 = jnp.bfloat16


def mm(a, b):
    return jnp.dot(a, b, preferred_element_type=F32)


def attend_kernel(
    rank_ref, len_ref, plan_ref, q_own, g_own, q_lent, g_lent, kv_ref, o_ref, dq_ref, dkv_ref,
    inv_ref, end_ref, first_ref, last_ref, s_ref, p_ref, kv_buf, acc_kv, zeros, q_ref, g_ref,
    qt_ref, gt_ref, gs_ref, m_ref, acc_ref, dqt_ref, load_sem, store_sem, zero_sem, q_sem,
):
    n_blocks = plan_ref.shape[0]
    n_tiles = n_blocks * (BLK // KT)
    rank = rank_ref[0]
    core = rank % 2

    def side_of(u):
        return (u % 2 + core) % 2

    def fetch(u):
        if u < 2:
            rows = pl.ds(pl.multiple_of((u * 2 + side_of(u)) * ROWS, ROWS), ROWS)
            pair = (q_own, g_own)
        else:
            rows = pl.ds((u - 2) * ROWS, ROWS)
            pair = (q_lent, g_lent)
        into = pl.ds(u * ROWS, ROWS)
        return [
            pltpu.make_async_copy(source.at[rows, :], target.at[into, :], q_sem.at[u, a])
            for a, (source, target) in enumerate(zip(pair, (q_ref, g_ref)))
        ]

    fetches = [fetch(u) for u in range(TILES)]
    for copies in fetches:
        for copy in copies:
            copy.start()

    def invert(i, c):
        inv_ref[plan_ref[i]] = i
        return c

    lax.fori_loop(0, n_blocks, invert, 0)
    end_ref[0] = 0
    for d in range(NDOC):
        end_ref[d + 1] = end_ref[d] + len_ref[d]

    def start_of(position):
        first = jnp.int32(0)
        for d in range(1, NDOC):
            first = jnp.where(position >= end_ref[d], end_ref[d], first)
        return first

    def pos_of(u):
        holder = jnp.where(u < 2, rank, rank + 1 - 2 * core)
        return plan_ref[holder * 2 + u % 2] * BLK + side_of(u) * QT

    def home(kt, j):
        rb = inv_ref[kt // 2]
        base = (rb // 2) * (2 * PER) + j * PER + (rb % 2) * BLK + (kt % 2) * KT
        return pl.ds(pl.multiple_of(base, KT), KT)

    def load(kt, j):
        return pltpu.make_async_copy(kv_ref.at[home(kt, j), :], kv_buf.at[kt, j], load_sem.at[kt, j])

    def store(kt, j):
        return pltpu.make_async_copy(kv_buf.at[kt, j], dkv_ref.at[home(kt, j), :], store_sem.at[kt, j])

    def blank(kt, j):
        return pltpu.make_async_copy(zeros, dkv_ref.at[home(kt, j), :], zero_sem)

    def over(u, action, mark=None):
        pos0 = pos_of(u)

        def body(kt, c):
            if mark is None:
                action(kt)
            else:
                pl.when(mark[kt] == u)(lambda: action(kt))
            return c

        lax.fori_loop(start_of(pos0) // KT, pos0 // KT + 1, body, 0)

    def begin(kt):
        for j in (0, 1):
            load(kt, j).start()

    def clear(kt):
        acc_kv[kt] = jnp.zeros((2, KT, DH), F32)

    def ready(kt):
        for j in (0, 1):
            load(kt, j).wait()

    def finish(kt):
        kv_buf[kt, 0] = (acc_kv[kt, 0] * SCALE).astype(BF16)
        kv_buf[kt, 1] = acc_kv[kt, 1].astype(BF16)
        for j in (0, 1):
            store(kt, j).start()

    def stored(kt):
        for j in (0, 1):
            store(kt, j).wait()

    def blanks(act):
        def body(kt, c):
            @pl.when(first_ref[kt] == TILES)
            def _():
                for j in (0, 1):
                    act(blank(kt, j))

            return c

        lax.fori_loop(0, n_tiles, body, 0)

    def unmark(kt, c):
        first_ref[kt] = TILES
        last_ref[kt] = TILES
        return c

    lax.fori_loop(0, n_tiles, unmark, 0)
    for u in range(TILES):

        def mark(kt, u=u):
            last_ref[kt] = u
            first_ref[kt] = jnp.minimum(first_ref[kt], u)

        over(u, mark)
        over(u, begin, first_ref)
    zeros[...] = jnp.zeros(zeros.shape, BF16)
    for u in range(TILES):
        over(u, clear, first_ref)
    blanks(lambda copy: copy.start())

    def tile(u, c):
        pos0 = pos_of(u)
        rows = pl.ds(pl.multiple_of(u * ROWS, ROWS), ROWS)
        last = pos0 // KT
        first = start_of(pos0) // KT
        full_from = start_of(pos0 + QT - 1)
        count = last - first + 1
        q_pos = pos0 + lax.broadcasted_iota(jnp.int32, (1, ROWS), 1) // GROUP
        q_lo = jnp.zeros((1, ROWS), jnp.int32)
        for d in range(1, NDOC):
            q_lo = jnp.where(q_pos >= end_ref[d], end_ref[d], q_lo)
        for a, (source, target) in enumerate(((q_lent, q_ref), (g_lent, g_ref))):
            pltpu.make_async_copy(source.at[pl.ds(0, ROWS), :], target.at[rows, :], q_sem.at[u, a]).wait()
        over(u, ready, first_ref)
        qt_ref[...] = q_ref[rows, :].T
        m_ref[...] = jnp.full(m_ref.shape, NEG, F32)
        acc_ref[...] = jnp.zeros(acc_ref.shape, F32)
        dqt_ref[...] = jnp.zeros(dqt_ref.shape, F32)

        def here(t):
            return pl.ds(pl.multiple_of(t * KT, KT), KT)

        def each(body):
            def run(i, c):
                body(i * UNROLL, UNROLL)
                return c

            lax.fori_loop(0, count // UNROLL, run, 0)
            if UNROLL == 2:
                pl.when(count % 2 == 1)(lambda: body(count - 1, 1))

        def scores(t0, n):
            kt0 = first + t0
            whole = (kt0 + (n - 1) < last) & (kt0 * KT >= full_from)

            def go(masked):
                top = m_ref[...]
                for i in range(n):
                    s = mm(kv_buf[kt0 + i, 0], qt_ref[...]) * CONST
                    if masked:
                        k_pos = (kt0 + i) * KT + lax.broadcasted_iota(jnp.int32, (KT, 1), 0)
                        s = jnp.where((k_pos >= q_lo) & (k_pos <= q_pos), s, NEG)
                    s_ref[here(t0 + i), :] = s
                    top = jnp.maximum(top, jnp.max(s.reshape(KT // 8, 8, ROWS), axis=0))
                m_ref[...] = top

            pl.when(whole)(lambda: go(False))
            pl.when(jnp.logical_not(whole))(lambda: go(True))

        each(scores)
        m_ref[0:1, :] = jnp.max(m_ref[...], axis=0, keepdims=True)

        def outputs(t0, n):
            total = acc_ref[...]
            for i in range(n):
                v = kv_buf[first + t0 + i, 1]
                vt = jnp.concatenate([v.T, jnp.ones((16, KT), BF16)], axis=0)
                p = jnp.exp2(s_ref[here(t0 + i), :] - m_ref[0:1, :]).astype(BF16)
                p_ref[here(t0 + i), :] = p
                total = total + mm(vt, p)
            acc_ref[...] = total

        each(outputs)
        inv_sum = 1.0 / acc_ref[DH : DH + 1, :]
        out_t = (acc_ref[0:DH, :] * inv_sum).astype(BF16)
        o_ref[rows, :] = out_t.T
        g_t = (g_ref[rows, :].T.astype(F32) * inv_sum).astype(BF16)
        gt_ref[...] = g_t
        gs_ref[...] = g_t.T
        m_ref[1:2, :] = jnp.sum(out_t.astype(F32) * g_t.astype(F32), axis=0, keepdims=True)

        def grads(t0, n):
            for i in range(n):
                slot = first + t0 + i
                k = kv_buf[slot, 0]
                p = p_ref[here(t0 + i), :]
                acc_kv[slot, 1] += mm(p, gs_ref[...])
                dp = mm(kv_buf[slot, 1], gt_ref[...])
                ds = (p.astype(F32) * (dp - m_ref[1:2, :])).astype(BF16)
                acc_kv[slot, 0] += mm(ds, q_ref[rows, :])
                dqt_ref[...] += mm(k.T, ds)

        each(grads)
        dq_ref[rows, :] = (dqt_ref[...] * SCALE).astype(BF16).T
        over(u, finish, last_ref)
        return c

    lax.fori_loop(0, TILES, tile, 0)
    blanks(lambda copy: copy.wait())
    for u in range(TILES):
        over(u, stored, last_ref)


def attend(rank, doc_lengths, block_plan, q, g, q_lent, g_lent, kv):
    n_rows = q.shape[0]
    n_kv = kv.shape[0]
    n_tiles = n_kv // (2 * KT)
    smem = pl.BlockSpec(memory_space=pltpu.SMEM)
    vmem = pl.BlockSpec(memory_space=pltpu.VMEM)
    hbm = pl.BlockSpec(memory_space=pl.ANY)
    dma = pltpu.SemaphoreType.DMA
    return pl.pallas_call(
        attend_kernel,
        out_shape=(
            jax.ShapeDtypeStruct((n_rows, DH), BF16),
            jax.ShapeDtypeStruct((n_rows, DH), BF16),
            jax.ShapeDtypeStruct((n_kv, DH), BF16),
        ),
        in_specs=[smem, smem, smem, hbm, hbm, hbm, hbm, hbm],
        out_specs=(vmem, vmem, hbm),
        scratch_shapes=[
            pltpu.SMEM((block_plan.shape[0],), jnp.int32),
            pltpu.SMEM((NDOC + 1,), jnp.int32),
            pltpu.SMEM((n_tiles,), jnp.int32),
            pltpu.SMEM((n_tiles,), jnp.int32),
            pltpu.VMEM((MAXT * KT, ROWS), F32),
            pltpu.VMEM((MAXT * KT, ROWS), BF16),
            pltpu.VMEM((n_tiles, 2, KT, DH), BF16),
            pltpu.VMEM((n_tiles, 2, KT, DH), F32),
            pltpu.VMEM((KT, DH), BF16),
            pltpu.VMEM((TILES * ROWS, DH), BF16),
            pltpu.VMEM((TILES * ROWS, DH), BF16),
            pltpu.VMEM((DH, ROWS), BF16),
            pltpu.VMEM((DH, ROWS), BF16),
            pltpu.VMEM((ROWS, DH), BF16),
            pltpu.VMEM((8, ROWS), F32),
            pltpu.VMEM((DH + 16, ROWS), F32),
            pltpu.VMEM((DH, ROWS), F32),
            dma((n_tiles, 2)),
            dma((n_tiles, 2)),
            dma,
            dma((TILES, 2)),
        ],
        compiler_params=pltpu.CompilerParams(vmem_limit_bytes=67043328),
    )(rank, doc_lengths, block_plan, q, g, q_lent, g_lent, kv)


MESH = pl.DeviceIdType.MESH
NZ = 4
HALF = PER // 2


def place():
    me = lax.axis_index("ctx")
    core = me % 2
    z = (me // 2) % NZ
    x = me // (2 * NZ)

    def at(dx, dz, dc):
        return (((x + dx) % 2) * NZ + (z + dz) % NZ) * 2 + (core + dc) % 2

    return at, core


def meet(peers):
    barrier = pltpu.get_barrier_semaphore()
    for peer in peers:
        pl.semaphore_signal(barrier, inc=1, device_id={"ctx": peer}, device_id_type=MESH)
    pl.semaphore_wait(barrier, len(peers))


def arrive(ref, sem):
    pltpu.make_async_copy(ref, ref, sem).wait()


class Outbox:
    def __init__(self, sems):
        self.sems = sems
        self.copies = []

    def send(self, source, target_ref, sem, target):
        copy = pltpu.make_async_remote_copy(
            src_ref=source,
            dst_ref=target_ref,
            send_sem=self.sems.at[len(self.copies)],
            recv_sem=sem,
            device_id={"ctx": target},
            device_id_type=MESH,
        )
        copy.start()
        self.copies.append(copy)

    def drain(self):
        for copy in self.copies:
            copy.wait_send()


def gather_kernel(
    k_ref, v_ref, q_ref, g_ref, out_ref, qx_ref, gx_ref, own_sem, send_sem, recv_sem, swap_sem
):
    at, core = place()
    me, other, up, down, twin = at(0, 0, 0), at(1, 0, 0), at(0, 1, 0), at(0, NZ - 1, 0), at(0, 0, 1)
    meet((other, up, down, twin))
    box = Outbox(send_sem)

    def slot(owner, j, h):
        return out_ref.at[pl.ds(pl.multiple_of(owner * (2 * PER) + j * PER + h * HALF, HALF), HALF), :]

    def sem(owner, j, h):
        return recv_sem.at[owner * 4 + j * 2 + h]

    def own(j, h):
        return (k_ref, v_ref)[j].at[pl.ds(h * HALF, HALF), :]

    def push(j, h, targets):
        for target in targets:
            box.send(own(j, h), slot(me, j, h), sem(me, j, h), target)

    push(1, 0, (up, down))
    push(0, 0, (other,))
    push(1, 1, (up, down))
    push(0, 1, (other,))
    push(0, 0, (up, down))
    push(1, 0, (other,))
    push(0, 1, (up, down))
    push(1, 1, (other,))
    for i in (0, 1):
        rows = pl.ds(pl.multiple_of((i * 2 + (i + core + 1) % 2) * PER, PER), PER)
        into = pl.ds(i * PER, PER)
        box.send(q_ref.at[rows, :], qx_ref.at[into, :], swap_sem.at[i], twin)
        box.send(g_ref.at[rows, :], gx_ref.at[into, :], swap_sem.at[2 + i], twin)
    keep = []
    for j in (0, 1):
        for h in (0, 1):
            push(j, h, (twin,))
            keep.append(pltpu.make_async_copy(own(j, h), slot(me, j, h), own_sem.at[j * 2 + h]))
            keep[-1].start()

    def relay(dx, dz, j, h, targets):
        owner = at(dx, dz, 0)
        arrive(slot(owner, j, h), sem(owner, j, h))
        for target in targets:
            box.send(slot(owner, j, h), slot(owner, j, h), sem(owner, j, h), target)

    relay(0, 3, 1, 0, (up, other, twin))
    relay(0, 1, 1, 0, (other, twin))
    relay(1, 0, 0, 0, (up, down, twin))
    relay(0, 3, 1, 1, (other, twin))
    relay(0, 1, 1, 1, (down, other, twin))
    relay(1, 0, 0, 1, (up, down, twin))
    relay(0, 3, 0, 0, (up, twin))
    relay(0, 1, 0, 0, (twin,))
    relay(1, 0, 1, 0, (twin,))
    relay(0, 3, 0, 1, (twin,))
    relay(0, 1, 0, 1, (down, twin))
    relay(1, 0, 1, 1, (twin,))
    relay(0, 2, 1, 0, (other, twin))
    relay(0, 2, 1, 1, (other, twin))
    relay(1, 3, 0, 0, (up, twin))
    relay(1, 1, 0, 0, (twin,))
    relay(1, 3, 0, 1, (twin,))
    relay(1, 1, 0, 1, (down, twin))
    for dz in (3, 1):
        for h in (0, 1):
            relay(1, dz, 1, h, (twin,))
    for h in (0, 1):
        relay(0, 2, 0, h, (twin,))
    for h in (0, 1):
        relay(1, 2, 0, h, (twin,))
    for h in (0, 1):
        relay(1, 2, 1, h, (twin,))
    for dx in (0, 1):
        for dz in range(NZ):
            owner = at(dx, dz, 1)
            for j in (0, 1):
                for h in (0, 1):
                    arrive(slot(owner, j, h), sem(owner, j, h))
    for i in (0, 1):
        into = pl.ds(i * PER, PER)
        arrive(qx_ref.at[into, :], swap_sem.at[i])
        arrive(gx_ref.at[into, :], swap_sem.at[2 + i])
    for copy in keep:
        copy.wait()
    box.drain()


def gather(k, v, q, g, n_ctx):
    vmem = pl.BlockSpec(memory_space=pltpu.VMEM)
    hbm = pl.BlockSpec(memory_space=pl.ANY)
    dma = pltpu.SemaphoreType.DMA
    return pl.pallas_call(
        gather_kernel,
        out_shape=(
            jax.ShapeDtypeStruct((n_ctx * 2 * PER, DH), BF16),
            jax.ShapeDtypeStruct((2 * PER, DH), BF16),
            jax.ShapeDtypeStruct((2 * PER, DH), BF16),
        ),
        in_specs=[vmem, vmem, hbm, hbm],
        out_specs=(hbm, hbm, hbm),
        scratch_shapes=[dma((4,)), dma((80,)), dma((4 * n_ctx,)), dma((4,))],
        compiler_params=pltpu.CompilerParams(
            collective_id=1, has_side_effects=True, vmem_limit_bytes=67043328
        ),
    )(k, v, q, g)


ORDER = (
    (1, 1, 2), (0, 1, 2), (1, 1, 1), (0, 1, 1), (0, 1, 3), (1, 1, 3), (0, 0, 2), (1, 1, 0),
    (0, 0, 1), (0, 0, 3), (1, 0, 2), (1, 0, 1), (1, 0, 3), (0, 1, 0), (1, 0, 0), (0, 0, 0),
)


def reduce_kernel(
    part_ref, o_ref, dq_ref, out_ref, gq_ref, dk_ref, dv_ref, mine, sib, rel, zin, xin,
    load_sem, send_sem, sib_sem, rel_sem, zin_sem, xin_sem, swap_sem, keep_sem,
):
    at, core = place()
    other, up, down, twin = at(1, 0, 0), at(0, 1, 0), at(0, NZ - 1, 0), at(0, 0, 1)
    meet((other, up, down, twin))
    box = Outbox(send_sem)

    def rows_of(j, owner):
        return part_ref.at[pl.ds(pl.multiple_of(owner * (2 * PER) + j * PER, PER), PER), :]

    loads = []
    for n, (j, dx, dz) in enumerate(ORDER):
        box.send(rows_of(j, at(dx, dz, 1)), sib.at[n], sib_sem.at[n], twin)
        loads.append(pltpu.make_async_copy(rows_of(j, at(dx, dz, 0)), mine.at[n], load_sem.at[n]))
        loads[n].start()
    keep = []
    for a, (source, target) in enumerate(((o_ref, out_ref), (dq_ref, gq_ref))):
        for i in (0, 1):
            kept = pl.ds(pl.multiple_of((i * 2 + (i + core) % 2) * PER, PER), PER)
            keep.append(
                pltpu.make_async_copy(source.at[pl.ds(i * PER, PER), :], target.at[kept, :], keep_sem.at[a, i])
            )
            keep[-1].start()
            box.send(
                source.at[pl.ds((2 + i) * PER, PER), :], target.at[kept, :], swap_sem.at[a, i], twin
            )

    def total(target, others, count):
        step = 256

        def body(i, c):
            rows = pl.ds(pl.multiple_of(i * step, step), step)
            value = others[0][rows, :].astype(F32)
            for ref in others[1:]:
                value = value + ref[rows, :].astype(F32)
            target[rows, :] = value.astype(BF16)
            return c

        lax.fori_loop(0, count // step, body, 0)

    def half(ref, h):
        return ref.at[pl.ds(h * HALF, HALF), :]

    def pair(j, dx, dz):
        n = ORDER.index((j, dx, dz))
        loads[n].wait()
        arrive(sib.at[n], sib_sem.at[n])
        return mine.at[n], sib.at[n]

    def joined(j, dx, dz, extra=()):
        a, b = pair(j, dx, dz)
        total(a, [a, b, *extra], PER)
        return a

    def across(j, dz):
        arrive(xin.at[dz], xin_sem.at[dz])
        return xin.at[dz]

    def far(cat, piece):
        box.send(half(piece, 0), rel.at[cat, 0], rel_sem.at[cat, 0], up)
        box.send(half(piece, 1), rel.at[cat, 1], rel_sem.at[cat, 1], down)

    def zsend(cat, side, h, piece):
        box.send(half(piece, h), half(zin.at[cat, side], h), zin_sem.at[cat, side, h], (up, down)[side])

    def pass_on(cat, above, below):
        arrive(rel.at[cat, 0], rel_sem.at[cat, 0])
        total(half(above, 0), [half(above, 0), rel.at[cat, 0]], HALF)
        zsend(cat, 0, 0, above)
        arrive(rel.at[cat, 1], rel_sem.at[cat, 1])
        total(half(below, 1), [half(below, 1), rel.at[cat, 1]], HALF)
        zsend(cat, 1, 1, below)

    def sides(cat):
        for h in (1, 0):
            for side in (0, 1):
                arrive(half(zin.at[cat, side], h), zin_sem.at[cat, side, h])
        return [zin.at[cat, 0], zin.at[cat, 1]]

    def cross(dz):
        box.send(joined(1, 1, dz), xin.at[dz], xin_sem.at[dz], other)

    cross(2)
    far(0, joined(0, 1, 2))
    cross(1)
    above = joined(0, 1, 1)
    zsend(0, 0, 1, above)
    below = joined(0, 1, 3)
    zsend(0, 1, 0, below)
    cross(3)
    pass_on(0, above, below)
    far(1, joined(0, 0, 2))
    cross(0)
    above = joined(0, 0, 1)
    zsend(1, 0, 1, above)
    below = joined(0, 0, 3)
    zsend(1, 1, 0, below)
    far(2, joined(1, 0, 2, (across(1, 2),)))
    pass_on(1, above, below)
    above = joined(1, 0, 1, (across(1, 1),))
    zsend(2, 0, 1, above)
    below = joined(1, 0, 3, (across(1, 3),))
    zsend(2, 1, 0, below)
    box.send(joined(0, 1, 0, sides(0)), xin.at[NZ], xin_sem.at[NZ], other)
    pass_on(2, above, below)
    near = pair(1, 0, 0)
    total(dv_ref, [*near, across(1, 0), *sides(2)], PER)
    near = pair(0, 0, 0)
    near = [*near, *sides(1)]
    total(dk_ref, [*near, across(0, NZ)], PER)
    for copy in keep:
        copy.wait()
    for a, target in enumerate((out_ref, gq_ref)):
        for i in (0, 1):
            lent = pl.ds(pl.multiple_of((i * 2 + (i + core + 1) % 2) * PER, PER), PER)
            arrive(target.at[lent, :], swap_sem.at[a, i])
    box.drain()


def reduce(part, o, dq):
    vmem = pl.BlockSpec(memory_space=pltpu.VMEM)
    hbm = pl.BlockSpec(memory_space=pl.ANY)
    dma = pltpu.SemaphoreType.DMA
    small = jax.ShapeDtypeStruct((PER, DH), BF16)
    large = jax.ShapeDtypeStruct(o.shape, BF16)
    return pl.pallas_call(
        reduce_kernel,
        out_shape=(large, large, small, small),
        in_specs=[hbm, hbm, hbm],
        out_specs=(vmem, vmem, vmem, vmem),
        scratch_shapes=[
            pltpu.VMEM((16, PER, DH), BF16),
            pltpu.VMEM((16, PER, DH), BF16),
            pltpu.VMEM((3, 2, HALF, DH), BF16),
            pltpu.VMEM((3, 2, PER, DH), BF16),
            pltpu.VMEM((NZ + 1, PER, DH), BF16),
            dma((16,)),
            dma((43,)),
            dma((16,)),
            dma((3, 2)),
            dma((3, 2, 2)),
            dma((NZ + 1,)),
            dma((2, 2)),
            dma((2, 2)),
        ],
        compiler_params=pltpu.CompilerParams(
            collective_id=2, has_side_effects=True, vmem_limit_bytes=67043328
        ),
    )(part, o, dq)


def shards(queries, keys, values, grad_out, doc_lengths, block_plan):
    tok = queries.shape[0]
    n_ctx = lax.axis_size("ctx")
    rank = lax.axis_index("ctx").astype(jnp.int32).reshape(1)
    q = queries.reshape(tok * GROUP, DH)
    g = grad_out.reshape(tok * GROUP, DH)
    kv, q_lent, g_lent = gather(keys.reshape(tok, DH), values.reshape(tok, DH), q, g, n_ctx)
    out, dq, part = attend(rank, doc_lengths, block_plan, q, g, q_lent, g_lent, kv)
    out, dq, dk, dv = reduce(part, out, dq)
    return (
        out.reshape(tok, GROUP, DH),
        dq.reshape(tok, GROUP, DH),
        dk.reshape(tok, 1, DH),
        dv.reshape(tok, 1, DH),
    )


def solution(mesh):
    split = P("ctx", "head", None)
    return jax.shard_map(
        shards,
        mesh=mesh,
        in_specs=(split, split, split, split, P(), P()),
        out_specs=(split, split, split, split),
        check_vma=False,
    )
```

```python
import math

import jax
import jax.numpy as jnp
from jax import lax
from jax.experimental import pallas as pl
from jax.experimental.pallas import tpu as pltpu
from jax.sharding import PartitionSpec as P

DH = 128
GROUP = 4
BLK = 512
DOC_MOST = 4096
NDOC = 8
QT = 256
ROWS = QT * GROUP
KT = 256
UNROLL = 4
MAXT = (DOC_MOST + QT) // KT
TILES = 4
PER = 1024
NEG = -1e30
SCALE = 1.0 / math.sqrt(DH)
CONST = SCALE * math.log2(math.e)
F32 = jnp.float32
BF16 = jnp.bfloat16


def mm(a, b):
    return jnp.dot(a, b, preferred_element_type=F32)


def attend_kernel(
    rank_ref, len_ref, plan_ref, q_own, g_own, q_lent, g_lent, kv_ref, o_ref, dq_ref, dkv_ref,
    inv_ref, end_ref, first_ref, last_ref, s_ref, p_ref, kv_buf, acc_kv, zeros, q_ref, g_ref,
    qt_ref, gt_ref, gs_ref, m_ref, acc_ref, dqt_ref, load_sem, store_sem, zero_sem, q_sem, o_buf, dq_buf, give_sem,
):
    n_blocks = plan_ref.shape[0]
    n_tiles = n_blocks * (BLK // KT)
    rank = rank_ref[0]
    core = rank % 2

    def side_of(u):
        return (u % 2 + core) % 2

    def fetch(u):
        if u < 2:
            rows = pl.ds(pl.multiple_of((u * 2 + side_of(u)) * ROWS, ROWS), ROWS)
            pair = (q_own, g_own)
        else:
            rows = pl.ds((u - 2) * ROWS, ROWS)
            pair = (q_lent, g_lent)
        into = pl.ds(u * ROWS, ROWS)
        return [
            pltpu.make_async_copy(source.at[rows, :], target.at[into, :], q_sem.at[u, a])
            for a, (source, target) in enumerate(zip(pair, (q_ref, g_ref)))
        ]

    fetches = [fetch(u) for u in range(TILES)]
    for copies in fetches:
        for copy in copies:
            copy.start()

    def invert(i, c):
        inv_ref[plan_ref[i]] = i
        return c

    lax.fori_loop(0, n_blocks, invert, 0)
    end_ref[0] = 0
    for d in range(NDOC):
        end_ref[d + 1] = end_ref[d] + len_ref[d]

    def start_of(position):
        first = jnp.int32(0)
        for d in range(1, NDOC):
            first = jnp.where(position >= end_ref[d], end_ref[d], first)
        return first

    def pos_of(u):
        holder = jnp.where(u < 2, rank, rank + 1 - 2 * core)
        return plan_ref[holder * 2 + u % 2] * BLK + side_of(u) * QT

    def home(kt, j):
        rb = inv_ref[kt // 2]
        base = (rb // 2) * (2 * PER) + j * PER + (rb % 2) * BLK + (kt % 2) * KT
        return pl.ds(pl.multiple_of(base, KT), KT)

    def load(kt, j):
        return pltpu.make_async_copy(kv_ref.at[home(kt, j), :], kv_buf.at[kt, j], load_sem.at[kt, j])

    def store(kt, j):
        return pltpu.make_async_copy(kv_buf.at[kt, j], dkv_ref.at[home(kt, j), :], store_sem.at[kt, j])

    def blank(kt, j):
        return pltpu.make_async_copy(zeros, dkv_ref.at[home(kt, j), :], zero_sem)

    def over(u, action, mark=None):
        pos0 = pos_of(u)

        def body(kt, c):
            if mark is None:
                action(kt)
            else:
                pl.when(mark[kt] == u)(lambda: action(kt))
            return c

        lax.fori_loop(start_of(pos0) // KT, pos0 // KT + 1, body, 0)

    def begin(kt):
        for j in (0, 1):
            load(kt, j).start()

    def clear(kt):
        acc_kv[kt] = jnp.zeros((2, KT, DH), F32)

    def ready(kt):
        for j in (0, 1):
            load(kt, j).wait()

    def finish(kt):
        kv_buf[kt, 0] = (acc_kv[kt, 0] * SCALE).astype(BF16)
        kv_buf[kt, 1] = acc_kv[kt, 1].astype(BF16)
        for j in (0, 1):
            store(kt, j).start()

    def stored(kt):
        for j in (0, 1):
            store(kt, j).wait()

    def blanks(act):
        def body(kt, c):
            @pl.when(first_ref[kt] == TILES)
            def _():
                for j in (0, 1):
                    act(blank(kt, j))

            return c

        lax.fori_loop(0, n_tiles, body, 0)

    def unmark(kt, c):
        first_ref[kt] = TILES
        last_ref[kt] = TILES
        return c

    lax.fori_loop(0, n_tiles, unmark, 0)
    for u in range(TILES):

        def mark(kt, u=u):
            last_ref[kt] = u
            first_ref[kt] = jnp.minimum(first_ref[kt], u)

        over(u, mark)
        over(u, begin, first_ref)
    zeros[...] = jnp.zeros(zeros.shape, BF16)
    for u in range(TILES):
        over(u, clear, first_ref)
    blanks(lambda copy: copy.start())

    def give(u, a):
        rows = pl.ds(pl.multiple_of(u * ROWS, ROWS), ROWS)
        source, target = ((o_buf, o_ref), (dq_buf, dq_ref))[a]
        return pltpu.make_async_copy(source.at[rows, :], target.at[rows, :], give_sem.at[u, a])

    def tile(u, c):
        pos0 = pos_of(u)
        rows = pl.ds(pl.multiple_of(u * ROWS, ROWS), ROWS)
        last = pos0 // KT
        first = start_of(pos0) // KT
        count = last - first + 1
        q_pos = pos0 + lax.broadcasted_iota(jnp.int32, (1, ROWS), 1) // GROUP
        q_lo = jnp.zeros((1, ROWS), jnp.int32)
        for d in range(1, NDOC):
            q_lo = jnp.where(q_pos >= end_ref[d], end_ref[d], q_lo)
        for a, (source, target) in enumerate(((q_lent, q_ref), (g_lent, g_ref))):
            pltpu.make_async_copy(source.at[pl.ds(0, ROWS), :], target.at[rows, :], q_sem.at[u, a]).wait()
        over(u, ready, first_ref)
        qt_ref[...] = q_ref[rows, :].T
        m_ref[...] = jnp.full(m_ref.shape, NEG, F32)
        acc_ref[...] = jnp.zeros(acc_ref.shape, F32)
        dqt_ref[...] = jnp.zeros(dqt_ref.shape, F32)

        def here(t):
            return pl.ds(pl.multiple_of(t * KT, KT), KT)

        def each(body, total):
            def run(i, c):
                body(i * UNROLL, UNROLL)
                return c

            lax.fori_loop(0, total // UNROLL, run, 0)
            for n in range(1, UNROLL):
                pl.when(total % UNROLL == n)(lambda n=n: body(total - n, n))

        def scores(t0, n, final=False):
            top = m_ref[...]
            for i in range(n):
                s = mm(kv_buf[first + t0 + i, 0], qt_ref[...]) * CONST
                k_pos = (first + t0 + i) * KT + lax.broadcasted_iota(jnp.int32, (KT, 1), 0)
                seen = k_pos >= q_lo
                if final:
                    seen = seen & (k_pos <= q_pos)
                s = jnp.where(seen, s, NEG)
                s_ref[here(t0 + i), :] = s
                top = jnp.maximum(top, jnp.max(s.reshape(KT // 8, 8, ROWS), axis=0))
            m_ref[...] = top

        each(scores, last - first)
        scores(last - first, 1, True)
        m_ref[0:1, :] = jnp.max(m_ref[...], axis=0, keepdims=True)

        def outputs(t0, n):
            total = acc_ref[...]
            for i in range(n):
                v = kv_buf[first + t0 + i, 1]
                vt = jnp.concatenate([v.T, jnp.ones((16, KT), BF16)], axis=0)
                p = jnp.exp2(s_ref[here(t0 + i), :] - m_ref[0:1, :]).astype(BF16)
                p_ref[here(t0 + i), :] = p
                total = total + mm(vt, p)
            acc_ref[...] = total

        each(outputs, count)
        inv_sum = 1.0 / acc_ref[DH : DH + 1, :]
        out_t = (acc_ref[0:DH, :] * inv_sum).astype(BF16)
        o_buf[rows, :] = out_t.T
        give(u, 0).start()
        g_t = (g_ref[rows, :].T.astype(F32) * inv_sum).astype(BF16)
        gt_ref[...] = g_t
        gs_ref[...] = g_t.T
        m_ref[1:2, :] = jnp.sum(out_t.astype(F32) * g_t.astype(F32), axis=0, keepdims=True)

        def grads(t0, n):
            for i in range(n):
                slot = first + t0 + i
                k = kv_buf[slot, 0]
                p = p_ref[here(t0 + i), :]
                acc_kv[slot, 1] += mm(p, gs_ref[...])
                dp = mm(kv_buf[slot, 1], gt_ref[...])
                ds = (p.astype(F32) * (dp - m_ref[1:2, :])).astype(BF16)
                acc_kv[slot, 0] += mm(ds, q_ref[rows, :])
                dqt_ref[...] += mm(k.T, ds)

        each(grads, count)
        dq_buf[rows, :] = (dqt_ref[...] * SCALE).astype(BF16).T
        give(u, 1).start()
        over(u, finish, last_ref)
        return c

    lax.fori_loop(0, TILES, tile, 0)
    blanks(lambda copy: copy.wait())
    for u in range(TILES):
        over(u, stored, last_ref)
        for a in (0, 1):
            give(u, a).wait()


def attend(rank, doc_lengths, block_plan, q, g, q_lent, g_lent, kv):
    n_rows = q.shape[0]
    n_kv = kv.shape[0]
    n_tiles = n_kv // (2 * KT)
    smem = pl.BlockSpec(memory_space=pltpu.SMEM)
    hbm = pl.BlockSpec(memory_space=pl.ANY)
    dma = pltpu.SemaphoreType.DMA
    return pl.pallas_call(
        attend_kernel,
        out_shape=(
            jax.ShapeDtypeStruct((n_rows, DH), BF16),
            jax.ShapeDtypeStruct((n_rows, DH), BF16),
            jax.ShapeDtypeStruct((n_kv, DH), BF16),
        ),
        in_specs=[smem, smem, smem, hbm, hbm, hbm, hbm, hbm],
        out_specs=(hbm, hbm, hbm),
        scratch_shapes=[
            pltpu.SMEM((block_plan.shape[0],), jnp.int32),
            pltpu.SMEM((NDOC + 1,), jnp.int32),
            pltpu.SMEM((n_tiles,), jnp.int32),
            pltpu.SMEM((n_tiles,), jnp.int32),
            pltpu.VMEM((MAXT * KT, ROWS), F32),
            pltpu.VMEM((MAXT * KT, ROWS), BF16),
            pltpu.VMEM((n_tiles, 2, KT, DH), BF16),
            pltpu.VMEM((n_tiles, 2, KT, DH), F32),
            pltpu.VMEM((KT, DH), BF16),
            pltpu.VMEM((TILES * ROWS, DH), BF16),
            pltpu.VMEM((TILES * ROWS, DH), BF16),
            pltpu.VMEM((DH, ROWS), BF16),
            pltpu.VMEM((DH, ROWS), BF16),
            pltpu.VMEM((ROWS, DH), BF16),
            pltpu.VMEM((8, ROWS), F32),
            pltpu.VMEM((DH + 16, ROWS), F32),
            pltpu.VMEM((DH, ROWS), F32),
            dma((n_tiles, 2)),
            dma((n_tiles, 2)),
            dma,
            dma((TILES, 2)),
            pltpu.VMEM((TILES * ROWS, DH), BF16),
            pltpu.VMEM((TILES * ROWS, DH), BF16),
            dma((TILES, 2)),
        ],
        compiler_params=pltpu.CompilerParams(vmem_limit_bytes=67043328),
    )(rank, doc_lengths, block_plan, q, g, q_lent, g_lent, kv)


MESH = pl.DeviceIdType.MESH
NZ = 4
HALF = PER // 2


def place():
    me = lax.axis_index("ctx")
    core = me % 2
    z = (me // 2) % NZ
    x = me // (2 * NZ)

    def at(dx, dz, dc):
        return (((x + dx) % 2) * NZ + (z + dz) % NZ) * 2 + (core + dc) % 2

    return at, core


def meet(peers):
    barrier = pltpu.get_barrier_semaphore()
    for peer in peers:
        pl.semaphore_signal(barrier, inc=1, device_id={"ctx": peer}, device_id_type=MESH)
    pl.semaphore_wait(barrier, len(peers))


def arrive(ref, sem):
    pltpu.make_async_copy(ref, ref, sem).wait()


class Outbox:
    def __init__(self, sems):
        self.sems = sems
        self.copies = []

    def send(self, source, target_ref, sem, target):
        copy = pltpu.make_async_remote_copy(
            src_ref=source,
            dst_ref=target_ref,
            send_sem=self.sems.at[len(self.copies)],
            recv_sem=sem,
            device_id={"ctx": target},
            device_id_type=MESH,
        )
        copy.start()
        self.copies.append(copy)

    def drain(self):
        for copy in self.copies:
            copy.wait_send()


def gather_kernel(
    k_ref, v_ref, q_ref, g_ref, out_ref, qx_ref, gx_ref, own_sem, send_sem, recv_sem, swap_sem
):
    at, core = place()
    me, other, up, down, twin = at(0, 0, 0), at(1, 0, 0), at(0, 1, 0), at(0, NZ - 1, 0), at(0, 0, 1)
    meet((other, up, down, twin))
    box = Outbox(send_sem)

    def slot(owner, j, h):
        return out_ref.at[pl.ds(pl.multiple_of(owner * (2 * PER) + j * PER + h * HALF, HALF), HALF), :]

    def sem(owner, j, h):
        return recv_sem.at[owner * 4 + j * 2 + h]

    def own(j, h):
        return (k_ref, v_ref)[j].at[pl.ds(h * HALF, HALF), :]

    def push(j, h, targets):
        for target in targets:
            box.send(own(j, h), slot(me, j, h), sem(me, j, h), target)

    push(1, 0, (up, down))
    push(0, 0, (other,))
    push(1, 1, (up, down))
    push(0, 1, (other,))
    push(0, 0, (up, down))
    push(1, 0, (other,))
    push(0, 1, (up, down))
    push(1, 1, (other,))
    for i in (0, 1):
        rows = pl.ds(pl.multiple_of((i * 2 + (i + core + 1) % 2) * PER, PER), PER)
        into = pl.ds(i * PER, PER)
        box.send(q_ref.at[rows, :], qx_ref.at[into, :], swap_sem.at[i], twin)
        box.send(g_ref.at[rows, :], gx_ref.at[into, :], swap_sem.at[2 + i], twin)
    keep = []
    for j in (0, 1):
        for h in (0, 1):
            push(j, h, (twin,))
            keep.append(pltpu.make_async_copy(own(j, h), slot(me, j, h), own_sem.at[j * 2 + h]))
            keep[-1].start()

    def relay(dx, dz, j, h, targets):
        owner = at(dx, dz, 0)
        arrive(slot(owner, j, h), sem(owner, j, h))
        for target in targets:
            box.send(slot(owner, j, h), slot(owner, j, h), sem(owner, j, h), target)

    relay(0, 3, 1, 0, (up, other, twin))
    relay(0, 1, 1, 0, (other, twin))
    relay(1, 0, 0, 0, (up, down, twin))
    relay(0, 3, 1, 1, (other, twin))
    relay(0, 1, 1, 1, (down, other, twin))
    relay(1, 0, 0, 1, (up, down, twin))
    relay(0, 3, 0, 0, (up, twin))
    relay(0, 1, 0, 0, (twin,))
    relay(1, 0, 1, 0, (twin,))
    relay(0, 3, 0, 1, (twin,))
    relay(0, 1, 0, 1, (down, twin))
    relay(1, 0, 1, 1, (twin,))
    relay(0, 2, 1, 0, (other, twin))
    relay(0, 2, 1, 1, (other, twin))
    relay(1, 3, 0, 0, (up, twin))
    relay(1, 1, 0, 0, (twin,))
    relay(1, 3, 0, 1, (twin,))
    relay(1, 1, 0, 1, (down, twin))
    for dz in (3, 1):
        for h in (0, 1):
            relay(1, dz, 1, h, (twin,))
    for h in (0, 1):
        relay(0, 2, 0, h, (twin,))
    for h in (0, 1):
        relay(1, 2, 0, h, (twin,))
    for h in (0, 1):
        relay(1, 2, 1, h, (twin,))
    for dx in (0, 1):
        for dz in range(NZ):
            owner = at(dx, dz, 1)
            for j in (0, 1):
                for h in (0, 1):
                    arrive(slot(owner, j, h), sem(owner, j, h))
    for i in (0, 1):
        into = pl.ds(i * PER, PER)
        arrive(qx_ref.at[into, :], swap_sem.at[i])
        arrive(gx_ref.at[into, :], swap_sem.at[2 + i])
    for copy in keep:
        copy.wait()
    box.drain()


def gather(k, v, q, g, n_ctx):
    hbm = pl.BlockSpec(memory_space=pl.ANY)
    dma = pltpu.SemaphoreType.DMA
    return pl.pallas_call(
        gather_kernel,
        out_shape=(
            jax.ShapeDtypeStruct((n_ctx * 2 * PER, DH), BF16),
            jax.ShapeDtypeStruct((2 * PER, DH), BF16),
            jax.ShapeDtypeStruct((2 * PER, DH), BF16),
        ),
        in_specs=[hbm, hbm, hbm, hbm],
        out_specs=(hbm, hbm, hbm),
        scratch_shapes=[dma((4,)), dma((80,)), dma((4 * n_ctx,)), dma((4,))],
        compiler_params=pltpu.CompilerParams(
            collective_id=1, has_side_effects=True, vmem_limit_bytes=67043328
        ),
    )(k, v, q, g)


ORDER = (
    (1, 1, 2), (0, 1, 2), (1, 1, 1), (0, 1, 1), (0, 1, 3), (1, 1, 3), (0, 0, 2), (1, 1, 0),
    (0, 0, 1), (0, 0, 3), (1, 0, 2), (1, 0, 1), (1, 0, 3), (0, 1, 0), (1, 0, 0), (0, 0, 0),
)


def reduce_kernel(
    part_ref, o_ref, dq_ref, out_ref, gq_ref, dk_ref, dv_ref, mine, sib, rel, zin, xin,
    load_sem, send_sem, sib_sem, rel_sem, zin_sem, xin_sem, swap_sem, keep_sem,
):
    at, core = place()
    other, up, down, twin = at(1, 0, 0), at(0, 1, 0), at(0, NZ - 1, 0), at(0, 0, 1)
    meet((other, up, down, twin))
    box = Outbox(send_sem)

    def rows_of(j, owner):
        return part_ref.at[pl.ds(pl.multiple_of(owner * (2 * PER) + j * PER, PER), PER), :]

    loads = []
    for n, (j, dx, dz) in enumerate(ORDER):
        box.send(rows_of(j, at(dx, dz, 1)), sib.at[n], sib_sem.at[n], twin)
        loads.append(pltpu.make_async_copy(rows_of(j, at(dx, dz, 0)), mine.at[n], load_sem.at[n]))
        loads[n].start()
    keep = []
    for a, (source, target) in enumerate(((o_ref, out_ref), (dq_ref, gq_ref))):
        for i in (0, 1):
            kept = pl.ds(pl.multiple_of((i * 2 + (i + core) % 2) * PER, PER), PER)
            keep.append(
                pltpu.make_async_copy(source.at[pl.ds(i * PER, PER), :], target.at[kept, :], keep_sem.at[a, i])
            )
            keep[-1].start()
            box.send(
                source.at[pl.ds((2 + i) * PER, PER), :], target.at[kept, :], swap_sem.at[a, i], twin
            )

    def total(target, others, count):
        step = 256

        def body(i, c):
            rows = pl.ds(pl.multiple_of(i * step, step), step)
            value = others[0][rows, :].astype(F32)
            for ref in others[1:]:
                value = value + ref[rows, :].astype(F32)
            target[rows, :] = value.astype(BF16)
            return c

        lax.fori_loop(0, count // step, body, 0)

    def half(ref, h):
        return ref.at[pl.ds(h * HALF, HALF), :]

    def pair(j, dx, dz):
        n = ORDER.index((j, dx, dz))
        loads[n].wait()
        arrive(sib.at[n], sib_sem.at[n])
        return mine.at[n], sib.at[n]

    def joined(j, dx, dz, extra=()):
        a, b = pair(j, dx, dz)
        total(a, [a, b, *extra], PER)
        return a

    def across(j, dz):
        arrive(xin.at[dz], xin_sem.at[dz])
        return xin.at[dz]

    def far(cat, piece):
        box.send(half(piece, 0), rel.at[cat, 0], rel_sem.at[cat, 0], up)
        box.send(half(piece, 1), rel.at[cat, 1], rel_sem.at[cat, 1], down)

    def zsend(cat, side, h, piece):
        box.send(half(piece, h), half(zin.at[cat, side], h), zin_sem.at[cat, side, h], (up, down)[side])

    def pass_on(cat, above, below):
        arrive(rel.at[cat, 0], rel_sem.at[cat, 0])
        total(half(above, 0), [half(above, 0), rel.at[cat, 0]], HALF)
        zsend(cat, 0, 0, above)
        arrive(rel.at[cat, 1], rel_sem.at[cat, 1])
        total(half(below, 1), [half(below, 1), rel.at[cat, 1]], HALF)
        zsend(cat, 1, 1, below)

    def sides(cat):
        for h in (1, 0):
            for side in (0, 1):
                arrive(half(zin.at[cat, side], h), zin_sem.at[cat, side, h])
        return [zin.at[cat, 0], zin.at[cat, 1]]

    def cross(dz):
        box.send(joined(1, 1, dz), xin.at[dz], xin_sem.at[dz], other)

    cross(2)
    far(0, joined(0, 1, 2))
    cross(1)
    above = joined(0, 1, 1)
    zsend(0, 0, 1, above)
    below = joined(0, 1, 3)
    zsend(0, 1, 0, below)
    cross(3)
    pass_on(0, above, below)
    far(1, joined(0, 0, 2))
    cross(0)
    above = joined(0, 0, 1)
    zsend(1, 0, 1, above)
    below = joined(0, 0, 3)
    zsend(1, 1, 0, below)
    far(2, joined(1, 0, 2, (across(1, 2),)))
    pass_on(1, above, below)
    above = joined(1, 0, 1, (across(1, 1),))
    zsend(2, 0, 1, above)
    below = joined(1, 0, 3, (across(1, 3),))
    zsend(2, 1, 0, below)
    box.send(joined(0, 1, 0, sides(0)), xin.at[NZ], xin_sem.at[NZ], other)
    pass_on(2, above, below)
    near = pair(1, 0, 0)
    total(dv_ref, [*near, across(1, 0), *sides(2)], PER)
    near = pair(0, 0, 0)
    near = [*near, *sides(1)]
    total(dk_ref, [*near, across(0, NZ)], PER)
    for copy in keep:
        copy.wait()
    for a, target in enumerate((out_ref, gq_ref)):
        for i in (0, 1):
            lent = pl.ds(pl.multiple_of((i * 2 + (i + core + 1) % 2) * PER, PER), PER)
            arrive(target.at[lent, :], swap_sem.at[a, i])
    box.drain()


def reduce(part, o, dq):
    vmem = pl.BlockSpec(memory_space=pltpu.VMEM)
    hbm = pl.BlockSpec(memory_space=pl.ANY)
    dma = pltpu.SemaphoreType.DMA
    small = jax.ShapeDtypeStruct((PER, DH), BF16)
    large = jax.ShapeDtypeStruct(o.shape, BF16)
    return pl.pallas_call(
        reduce_kernel,
        out_shape=(large, large, small, small),
        in_specs=[hbm, hbm, hbm],
        out_specs=(vmem, vmem, vmem, vmem),
        scratch_shapes=[
            pltpu.VMEM((16, PER, DH), BF16),
            pltpu.VMEM((16, PER, DH), BF16),
            pltpu.VMEM((3, 2, HALF, DH), BF16),
            pltpu.VMEM((3, 2, PER, DH), BF16),
            pltpu.VMEM((NZ + 1, PER, DH), BF16),
            dma((16,)),
            dma((43,)),
            dma((16,)),
            dma((3, 2)),
            dma((3, 2, 2)),
            dma((NZ + 1,)),
            dma((2, 2)),
            dma((2, 2)),
        ],
        compiler_params=pltpu.CompilerParams(
            collective_id=2, has_side_effects=True, vmem_limit_bytes=67043328
        ),
    )(part, o, dq)


def deliver_kernel(*refs):
    n = (len(refs) - 2) // 3
    sources, targets, held, in_sem, out_sem = refs[:n], refs[n : 2 * n], refs[2 * n : 3 * n], refs[-2], refs[-1]
    step = HALF
    parts = [(i, r) for i in range(n) for r in range(0, sources[i].shape[0], step)]

    def copy(m, a, b, sem):
        i, r = parts[m]
        return pltpu.make_async_copy(a[i].at[pl.ds(r, step), :], b[i].at[pl.ds(r, step), :], sem.at[m])

    for m in range(len(parts)):
        copy(m, sources, held, in_sem).start()
    for m in range(len(parts)):
        copy(m, sources, held, in_sem).wait()
        copy(m, held, targets, out_sem).start()
    for m in range(len(parts)):
        copy(m, held, targets, out_sem).wait()


def deliver(*arrays):
    n = len(arrays)
    parts = sum(a.shape[0] // HALF for a in arrays)
    hbm = pl.BlockSpec(memory_space=pl.ANY)
    return pl.pallas_call(
        deliver_kernel,
        out_shape=tuple(jax.ShapeDtypeStruct(a.shape, a.dtype) for a in arrays),
        in_specs=[hbm] * n,
        out_specs=(hbm,) * n,
        scratch_shapes=[pltpu.VMEM(a.shape, a.dtype) for a in arrays]
        + [pltpu.SemaphoreType.DMA((parts,)), pltpu.SemaphoreType.DMA((parts,))],
        compiler_params=pltpu.CompilerParams(vmem_limit_bytes=67043328),
    )(*arrays)


def shards(queries, keys, values, grad_out, doc_lengths, block_plan):
    tok = queries.shape[0]
    n_ctx = lax.axis_size("ctx")
    rank = lax.axis_index("ctx").astype(jnp.int32).reshape(1)
    q = queries.reshape(tok * GROUP, DH)
    g = grad_out.reshape(tok * GROUP, DH)
    kv, q_lent, g_lent = gather(keys.reshape(tok, DH), values.reshape(tok, DH), q, g, n_ctx)
    out, dq, part = attend(rank, doc_lengths, block_plan, q, g, q_lent, g_lent, kv)
    out, dq, dk, dv = deliver(*reduce(part, out, dq))
    return (
        out.reshape(tok, GROUP, DH),
        dq.reshape(tok, GROUP, DH),
        dk.reshape(tok, 1, DH),
        dv.reshape(tok, 1, DH),
    )


def solution(mesh):
    split = P("ctx", "head", None)
    return jax.shard_map(
        shards,
        mesh=mesh,
        in_specs=(split, split, split, split, P(), P()),
        out_specs=(split, split, split, split),
        check_vma=False,
    )
```

```python
import math

import jax
import jax.numpy as jnp
from jax import lax
from jax.experimental import pallas as pl
from jax.experimental.pallas import tpu as pltpu
from jax.sharding import PartitionSpec as P

DH = 128
GROUP = 4
BLK = 512
DOC_MOST = 4096
NDOC = 8
QT = 256
ROWS = QT * GROUP
KT = 256
UNROLL = 4
MAXT = (DOC_MOST + QT) // KT
TILES = 4
PER = 1024
NEG = -1e30
SCALE = 1.0 / math.sqrt(DH)
CONST = SCALE * math.log2(math.e)
F32 = jnp.float32
BF16 = jnp.bfloat16


def mm(a, b):
    return jnp.dot(a, b, preferred_element_type=F32)


def attend_kernel(
    rank_ref, len_ref, plan_ref, q_own, g_own, q_lent, g_lent, kv_ref, o_ref, dq_ref, dkv_ref,
    inv_ref, end_ref, first_ref, last_ref, s_ref, p_ref, kv_buf, acc_kv, zeros, q_ref, g_ref,
    qt_ref, gt_ref, gs_ref, m_ref, acc_ref, dqt_ref, load_sem, store_sem, zero_sem, q_sem, o_buf, dq_buf, give_sem,
):
    n_blocks = plan_ref.shape[0]
    rank = rank_ref[0]
    core = rank % 2

    def side_of(u):
        return (u % 2 + core) % 2

    def fetch(u):
        if u < 2:
            rows = pl.ds(pl.multiple_of((u * 2 + side_of(u)) * ROWS, ROWS), ROWS)
            pair = (q_own, g_own)
        else:
            rows = pl.ds((u - 2) * ROWS, ROWS)
            pair = (q_lent, g_lent)
        into = pl.ds(u * ROWS, ROWS)
        return [
            pltpu.make_async_copy(source.at[rows, :], target.at[into, :], q_sem.at[u, a])
            for a, (source, target) in enumerate(zip(pair, (q_ref, g_ref)))
        ]

    fetches = [fetch(u) for u in range(TILES)]
    for copies in fetches:
        for copy in copies:
            copy.start()

    def invert(i, c):
        inv_ref[plan_ref[i]] = i
        return c

    lax.fori_loop(0, n_blocks, invert, 0)
    end_ref[0] = 0
    for d in range(NDOC):
        end_ref[d + 1] = end_ref[d] + len_ref[d]

    def start_of(position):
        first = jnp.int32(0)
        for d in range(1, NDOC):
            first = jnp.where(position >= end_ref[d], end_ref[d], first)
        return first

    def pos_of(u):
        holder = jnp.where(u < 2, rank, rank + 1 - 2 * core)
        return plan_ref[holder * 2 + u % 2] * BLK + side_of(u) * QT

    def home(kb, j):
        rb = inv_ref[kb]
        base = (rb // 2) * (2 * PER) + j * PER + (rb % 2) * BLK
        return pl.ds(pl.multiple_of(base, BLK), BLK)

    def part(kt):
        return kt // 2, pl.ds(pl.multiple_of((kt % 2) * KT, KT), KT)

    def load(kt, j):
        return pltpu.make_async_copy(kv_ref.at[home(kt, j), :], kv_buf.at[kt, j], load_sem.at[kt, j])

    def store(kt, j):
        return pltpu.make_async_copy(kv_buf.at[kt, j], dkv_ref.at[home(kt, j), :], store_sem.at[kt, j])

    def blank(kt, j):
        return pltpu.make_async_copy(zeros, dkv_ref.at[home(kt, j), :], zero_sem)

    def over(u, action, mark=None):
        pos0 = pos_of(u)

        def body(kt, c):
            if mark is None:
                action(kt)
            else:
                pl.when(mark[kt] == u)(lambda: action(kt))
            return c

        lax.fori_loop(start_of(pos0) // BLK, pos0 // BLK + 1, body, 0)

    def begin(kt):
        for j in (0, 1):
            load(kt, j).start()

    def clear(kt):
        acc_kv[kt] = jnp.zeros((2, BLK, DH), F32)

    def ready(kt):
        for j in (0, 1):
            load(kt, j).wait()

    def finish(kt):
        kv_buf[kt, 0] = (acc_kv[kt, 0] * SCALE).astype(BF16)
        kv_buf[kt, 1] = acc_kv[kt, 1].astype(BF16)
        for j in (0, 1):
            store(kt, j).start()

    def stored(kt):
        for j in (0, 1):
            store(kt, j).wait()

    def blanks(act):
        def body(kt, c):
            @pl.when(first_ref[kt] == TILES)
            def _():
                for j in (0, 1):
                    act(blank(kt, j))

            return c

        lax.fori_loop(0, n_blocks, body, 0)

    def unmark(kt, c):
        first_ref[kt] = TILES
        last_ref[kt] = TILES
        return c

    lax.fori_loop(0, n_blocks, unmark, 0)
    for u in range(TILES):

        def mark(kt, u=u):
            last_ref[kt] = u
            first_ref[kt] = jnp.minimum(first_ref[kt], u)

        over(u, mark)
        over(u, begin, first_ref)
    zeros[...] = jnp.zeros(zeros.shape, BF16)
    for u in range(TILES):
        over(u, clear, first_ref)
    blanks(lambda copy: copy.start())

    def give(u, a):
        rows = pl.ds(pl.multiple_of(u * ROWS, ROWS), ROWS)
        source, target = ((o_buf, o_ref), (dq_buf, dq_ref))[a]
        return pltpu.make_async_copy(source.at[rows, :], target.at[rows, :], give_sem.at[u, a])

    def tile(u, c):
        pos0 = pos_of(u)
        rows = pl.ds(pl.multiple_of(u * ROWS, ROWS), ROWS)
        last = pos0 // KT
        first = start_of(pos0) // KT
        count = last - first + 1
        q_pos = pos0 + lax.broadcasted_iota(jnp.int32, (1, ROWS), 1) // GROUP
        q_lo = jnp.zeros((1, ROWS), jnp.int32)
        for d in range(1, NDOC):
            q_lo = jnp.where(q_pos >= end_ref[d], end_ref[d], q_lo)
        for a, (source, target) in enumerate(((q_lent, q_ref), (g_lent, g_ref))):
            pltpu.make_async_copy(source.at[pl.ds(0, ROWS), :], target.at[rows, :], q_sem.at[u, a]).wait()
        over(u, ready, first_ref)
        qt_ref[...] = q_ref[rows, :].T
        m_ref[...] = jnp.full(m_ref.shape, NEG, F32)
        acc_ref[...] = jnp.zeros(acc_ref.shape, F32)
        dqt_ref[...] = jnp.zeros(dqt_ref.shape, F32)

        def here(t):
            return pl.ds(pl.multiple_of(t * KT, KT), KT)

        def each(body, total):
            def run(i, c):
                body(i * UNROLL, UNROLL)
                return c

            lax.fori_loop(0, total // UNROLL, run, 0)
            for n in range(1, UNROLL):
                pl.when(total % UNROLL == n)(lambda n=n: body(total - n, n))

        def scores(t0, n, final=False):
            top = m_ref[...]
            for i in range(n):
                kb, at = part(first + t0 + i)
                s = mm(kv_buf[kb, 0, at, :], qt_ref[...]) * CONST
                k_pos = (first + t0 + i) * KT + lax.broadcasted_iota(jnp.int32, (KT, 1), 0)
                seen = k_pos >= q_lo
                if final:
                    seen = seen & (k_pos <= q_pos)
                s = jnp.where(seen, s, NEG)
                s_ref[here(t0 + i), :] = s
                top = jnp.maximum(top, jnp.max(s.reshape(KT // 8, 8, ROWS), axis=0))
            m_ref[...] = top

        each(scores, last - first)
        scores(last - first, 1, True)
        m_ref[0:1, :] = jnp.max(m_ref[...], axis=0, keepdims=True)

        def outputs(t0, n):
            total = acc_ref[...]
            for i in range(n):
                kb, at = part(first + t0 + i)
                v = kv_buf[kb, 1, at, :]
                vt = jnp.concatenate([v.T, jnp.ones((16, KT), BF16)], axis=0)
                p = jnp.exp2(s_ref[here(t0 + i), :] - m_ref[0:1, :]).astype(BF16)
                p_ref[here(t0 + i), :] = p
                total = total + mm(vt, p)
            acc_ref[...] = total

        each(outputs, count)
        inv_sum = 1.0 / acc_ref[DH : DH + 1, :]
        out_t = (acc_ref[0:DH, :] * inv_sum).astype(BF16)
        o_buf[rows, :] = out_t.T
        give(u, 0).start()
        g_t = (g_ref[rows, :].T.astype(F32) * inv_sum).astype(BF16)
        gt_ref[...] = g_t
        gs_ref[...] = g_t.T
        m_ref[1:2, :] = jnp.sum(out_t.astype(F32) * g_t.astype(F32), axis=0, keepdims=True)

        def grads(t0, n):
            for i in range(n):
                kb, at = part(first + t0 + i)
                k = kv_buf[kb, 0, at, :]
                p = p_ref[here(t0 + i), :]
                acc_kv[kb, 1, at, :] += mm(p, gs_ref[...])
                dp = mm(kv_buf[kb, 1, at, :], gt_ref[...])
                ds = (p.astype(F32) * (dp - m_ref[1:2, :])).astype(BF16)
                acc_kv[kb, 0, at, :] += mm(ds, q_ref[rows, :])
                dqt_ref[...] += mm(k.T, ds)

        each(grads, count)
        dq_buf[rows, :] = (dqt_ref[...] * SCALE).astype(BF16).T
        give(u, 1).start()
        over(u, finish, last_ref)
        return c

    lax.fori_loop(0, TILES, tile, 0)
    blanks(lambda copy: copy.wait())
    for u in range(TILES):
        over(u, stored, last_ref)
        for a in (0, 1):
            give(u, a).wait()


def attend(rank, doc_lengths, block_plan, q, g, q_lent, g_lent, kv):
    n_rows = q.shape[0]
    n_kv = kv.shape[0]
    n_blocks = n_kv // (2 * BLK)
    smem = pl.BlockSpec(memory_space=pltpu.SMEM)
    hbm = pl.BlockSpec(memory_space=pl.ANY)
    dma = pltpu.SemaphoreType.DMA
    return pl.pallas_call(
        attend_kernel,
        out_shape=(
            jax.ShapeDtypeStruct((n_rows, DH), BF16),
            jax.ShapeDtypeStruct((n_rows, DH), BF16),
            jax.ShapeDtypeStruct((n_kv, DH), BF16),
        ),
        in_specs=[smem, smem, smem, hbm, hbm, hbm, hbm, hbm],
        out_specs=(hbm, hbm, hbm),
        scratch_shapes=[
            pltpu.SMEM((block_plan.shape[0],), jnp.int32),
            pltpu.SMEM((NDOC + 1,), jnp.int32),
            pltpu.SMEM((n_blocks,), jnp.int32),
            pltpu.SMEM((n_blocks,), jnp.int32),
            pltpu.VMEM((MAXT * KT, ROWS), F32),
            pltpu.VMEM((MAXT * KT, ROWS), BF16),
            pltpu.VMEM((n_blocks, 2, BLK, DH), BF16),
            pltpu.VMEM((n_blocks, 2, BLK, DH), F32),
            pltpu.VMEM((BLK, DH), BF16),
            pltpu.VMEM((TILES * ROWS, DH), BF16),
            pltpu.VMEM((TILES * ROWS, DH), BF16),
            pltpu.VMEM((DH, ROWS), BF16),
            pltpu.VMEM((DH, ROWS), BF16),
            pltpu.VMEM((ROWS, DH), BF16),
            pltpu.VMEM((8, ROWS), F32),
            pltpu.VMEM((DH + 16, ROWS), F32),
            pltpu.VMEM((DH, ROWS), F32),
            dma((n_blocks, 2)),
            dma((n_blocks, 2)),
            dma,
            dma((TILES, 2)),
            pltpu.VMEM((TILES * ROWS, DH), BF16),
            pltpu.VMEM((TILES * ROWS, DH), BF16),
            dma((TILES, 2)),
        ],
        compiler_params=pltpu.CompilerParams(vmem_limit_bytes=67043328),
    )(rank, doc_lengths, block_plan, q, g, q_lent, g_lent, kv)


MESH = pl.DeviceIdType.MESH
NZ = 4
HALF = PER // 2


def place():
    me = lax.axis_index("ctx")
    core = me % 2
    z = (me // 2) % NZ
    x = me // (2 * NZ)

    def at(dx, dz, dc):
        return (((x + dx) % 2) * NZ + (z + dz) % NZ) * 2 + (core + dc) % 2

    return at, core


def meet(peers):
    barrier = pltpu.get_barrier_semaphore()
    for peer in peers:
        pl.semaphore_signal(barrier, inc=1, device_id={"ctx": peer}, device_id_type=MESH)
    pl.semaphore_wait(barrier, len(peers))


def arrive(ref, sem):
    pltpu.make_async_copy(ref, ref, sem).wait()


class Outbox:
    def __init__(self, sems):
        self.sems = sems
        self.copies = []

    def send(self, source, target_ref, sem, target):
        copy = pltpu.make_async_remote_copy(
            src_ref=source,
            dst_ref=target_ref,
            send_sem=self.sems.at[len(self.copies)],
            recv_sem=sem,
            device_id={"ctx": target},
            device_id_type=MESH,
        )
        copy.start()
        self.copies.append(copy)

    def drain(self):
        for copy in self.copies:
            copy.wait_send()


def gather_kernel(
    k_ref, v_ref, q_ref, g_ref, out_ref, qx_ref, gx_ref, own_sem, send_sem, recv_sem, swap_sem
):
    at, core = place()
    me, other, up, down, twin = at(0, 0, 0), at(1, 0, 0), at(0, 1, 0), at(0, NZ - 1, 0), at(0, 0, 1)
    meet((other, up, down, twin))
    box = Outbox(send_sem)

    def slot(owner, j, h):
        return out_ref.at[pl.ds(pl.multiple_of(owner * (2 * PER) + j * PER + h * HALF, HALF), HALF), :]

    def sem(owner, j, h):
        return recv_sem.at[owner * 4 + j * 2 + h]

    def own(j, h):
        return (k_ref, v_ref)[j].at[pl.ds(h * HALF, HALF), :]

    def push(j, h, targets):
        for target in targets:
            box.send(own(j, h), slot(me, j, h), sem(me, j, h), target)

    push(1, 0, (up, down))
    push(0, 0, (other,))
    push(1, 1, (up, down))
    push(0, 1, (other,))
    push(0, 0, (up, down))
    push(1, 0, (other,))
    push(0, 1, (up, down))
    push(1, 1, (other,))
    for i in (0, 1):
        rows = pl.ds(pl.multiple_of((i * 2 + (i + core + 1) % 2) * PER, PER), PER)
        into = pl.ds(i * PER, PER)
        box.send(q_ref.at[rows, :], qx_ref.at[into, :], swap_sem.at[i], twin)
        box.send(g_ref.at[rows, :], gx_ref.at[into, :], swap_sem.at[2 + i], twin)
    keep = []
    for j in (0, 1):
        for h in (0, 1):
            push(j, h, (twin,))
            keep.append(pltpu.make_async_copy(own(j, h), slot(me, j, h), own_sem.at[j * 2 + h]))
            keep[-1].start()

    def relay(dx, dz, j, h, targets):
        owner = at(dx, dz, 0)
        arrive(slot(owner, j, h), sem(owner, j, h))
        for target in targets:
            box.send(slot(owner, j, h), slot(owner, j, h), sem(owner, j, h), target)

    relay(0, 3, 1, 0, (up, other, twin))
    relay(0, 1, 1, 0, (other, twin))
    relay(1, 0, 0, 0, (up, down, twin))
    relay(0, 3, 1, 1, (other, twin))
    relay(0, 1, 1, 1, (down, other, twin))
    relay(1, 0, 0, 1, (up, down, twin))
    relay(0, 3, 0, 0, (up, twin))
    relay(0, 1, 0, 0, (twin,))
    relay(1, 0, 1, 0, (twin,))
    relay(0, 3, 0, 1, (twin,))
    relay(0, 1, 0, 1, (down, twin))
    relay(1, 0, 1, 1, (twin,))
    relay(0, 2, 1, 0, (other, twin))
    relay(0, 2, 1, 1, (other, twin))
    relay(1, 3, 0, 0, (up, twin))
    relay(1, 1, 0, 0, (twin,))
    relay(1, 3, 0, 1, (twin,))
    relay(1, 1, 0, 1, (down, twin))
    for dz in (3, 1):
        for h in (0, 1):
            relay(1, dz, 1, h, (twin,))
    for h in (0, 1):
        relay(0, 2, 0, h, (twin,))
    for h in (0, 1):
        relay(1, 2, 0, h, (twin,))
    for h in (0, 1):
        relay(1, 2, 1, h, (twin,))
    for dx in (0, 1):
        for dz in range(NZ):
            owner = at(dx, dz, 1)
            for j in (0, 1):
                for h in (0, 1):
                    arrive(slot(owner, j, h), sem(owner, j, h))
    for i in (0, 1):
        into = pl.ds(i * PER, PER)
        arrive(qx_ref.at[into, :], swap_sem.at[i])
        arrive(gx_ref.at[into, :], swap_sem.at[2 + i])
    for copy in keep:
        copy.wait()
    box.drain()


def gather(k, v, q, g, n_ctx):
    hbm = pl.BlockSpec(memory_space=pl.ANY)
    dma = pltpu.SemaphoreType.DMA
    return pl.pallas_call(
        gather_kernel,
        out_shape=(
            jax.ShapeDtypeStruct((n_ctx * 2 * PER, DH), BF16),
            jax.ShapeDtypeStruct((2 * PER, DH), BF16),
            jax.ShapeDtypeStruct((2 * PER, DH), BF16),
        ),
        in_specs=[hbm, hbm, hbm, hbm],
        out_specs=(hbm, hbm, hbm),
        scratch_shapes=[dma((4,)), dma((80,)), dma((4 * n_ctx,)), dma((4,))],
        compiler_params=pltpu.CompilerParams(
            collective_id=1, has_side_effects=True, vmem_limit_bytes=67043328
        ),
    )(k, v, q, g)


ORDER = (
    (1, 1, 2), (0, 1, 2), (1, 1, 1), (0, 1, 1), (0, 1, 3), (1, 1, 3), (0, 0, 2), (1, 1, 0),
    (0, 0, 1), (0, 0, 3), (1, 0, 2), (1, 0, 1), (1, 0, 3), (0, 1, 0), (1, 0, 0), (0, 0, 0),
)


def reduce_kernel(
    part_ref, o_ref, dq_ref, out_ref, gq_ref, dk_ref, dv_ref, mine, sib, rel, zin, xin,
    load_sem, send_sem, sib_sem, rel_sem, zin_sem, xin_sem, swap_sem, keep_sem,
):
    at, core = place()
    other, up, down, twin = at(1, 0, 0), at(0, 1, 0), at(0, NZ - 1, 0), at(0, 0, 1)
    meet((other, up, down, twin))
    box = Outbox(send_sem)

    def rows_of(j, owner):
        return part_ref.at[pl.ds(pl.multiple_of(owner * (2 * PER) + j * PER, PER), PER), :]

    loads = []
    for n, (j, dx, dz) in enumerate(ORDER):
        box.send(rows_of(j, at(dx, dz, 1)), sib.at[n], sib_sem.at[n], twin)
        loads.append(pltpu.make_async_copy(rows_of(j, at(dx, dz, 0)), mine.at[n], load_sem.at[n]))
        loads[n].start()
    keep = []
    for a, (source, target) in enumerate(((o_ref, out_ref), (dq_ref, gq_ref))):
        for i in (0, 1):
            kept = pl.ds(pl.multiple_of((i * 2 + (i + core) % 2) * PER, PER), PER)
            keep.append(
                pltpu.make_async_copy(source.at[pl.ds(i * PER, PER), :], target.at[kept, :], keep_sem.at[a, i])
            )
            keep[-1].start()
            box.send(
                source.at[pl.ds((2 + i) * PER, PER), :], target.at[kept, :], swap_sem.at[a, i], twin
            )

    def total(target, others, count):
        step = 256

        def body(i, c):
            rows = pl.ds(pl.multiple_of(i * step, step), step)
            value = others[0][rows, :].astype(F32)
            for ref in others[1:]:
                value = value + ref[rows, :].astype(F32)
            target[rows, :] = value.astype(BF16)
            return c

        lax.fori_loop(0, count // step, body, 0)

    def half(ref, h):
        return ref.at[pl.ds(h * HALF, HALF), :]

    def pair(j, dx, dz):
        n = ORDER.index((j, dx, dz))
        loads[n].wait()
        arrive(sib.at[n], sib_sem.at[n])
        return mine.at[n], sib.at[n]

    def joined(j, dx, dz, extra=()):
        a, b = pair(j, dx, dz)
        total(a, [a, b, *extra], PER)
        return a

    def across(j, dz):
        arrive(xin.at[dz], xin_sem.at[dz])
        return xin.at[dz]

    def far(cat, piece):
        box.send(half(piece, 0), rel.at[cat, 0], rel_sem.at[cat, 0], up)
        box.send(half(piece, 1), rel.at[cat, 1], rel_sem.at[cat, 1], down)

    def zsend(cat, side, h, piece):
        box.send(half(piece, h), half(zin.at[cat, side], h), zin_sem.at[cat, side, h], (up, down)[side])

    def pass_on(cat, above, below):
        arrive(rel.at[cat, 0], rel_sem.at[cat, 0])
        total(half(above, 0), [half(above, 0), rel.at[cat, 0]], HALF)
        zsend(cat, 0, 0, above)
        arrive(rel.at[cat, 1], rel_sem.at[cat, 1])
        total(half(below, 1), [half(below, 1), rel.at[cat, 1]], HALF)
        zsend(cat, 1, 1, below)

    def sides(cat):
        for h in (1, 0):
            for side in (0, 1):
                arrive(half(zin.at[cat, side], h), zin_sem.at[cat, side, h])
        return [zin.at[cat, 0], zin.at[cat, 1]]

    def cross(dz):
        box.send(joined(1, 1, dz), xin.at[dz], xin_sem.at[dz], other)

    cross(2)
    far(0, joined(0, 1, 2))
    cross(1)
    above = joined(0, 1, 1)
    zsend(0, 0, 1, above)
    below = joined(0, 1, 3)
    zsend(0, 1, 0, below)
    cross(3)
    pass_on(0, above, below)
    far(1, joined(0, 0, 2))
    cross(0)
    above = joined(0, 0, 1)
    zsend(1, 0, 1, above)
    below = joined(0, 0, 3)
    zsend(1, 1, 0, below)
    far(2, joined(1, 0, 2, (across(1, 2),)))
    pass_on(1, above, below)
    above = joined(1, 0, 1, (across(1, 1),))
    zsend(2, 0, 1, above)
    below = joined(1, 0, 3, (across(1, 3),))
    zsend(2, 1, 0, below)
    box.send(joined(0, 1, 0, sides(0)), xin.at[NZ], xin_sem.at[NZ], other)
    pass_on(2, above, below)
    near = pair(1, 0, 0)
    total(dv_ref, [*near, across(1, 0), *sides(2)], PER)
    near = pair(0, 0, 0)
    near = [*near, *sides(1)]
    total(dk_ref, [*near, across(0, NZ)], PER)
    for copy in keep:
        copy.wait()
    for a, target in enumerate((out_ref, gq_ref)):
        for i in (0, 1):
            lent = pl.ds(pl.multiple_of((i * 2 + (i + core + 1) % 2) * PER, PER), PER)
            arrive(target.at[lent, :], swap_sem.at[a, i])
    box.drain()


def reduce(part, o, dq):
    vmem = pl.BlockSpec(memory_space=pltpu.VMEM)
    hbm = pl.BlockSpec(memory_space=pl.ANY)
    dma = pltpu.SemaphoreType.DMA
    small = jax.ShapeDtypeStruct((PER, DH), BF16)
    large = jax.ShapeDtypeStruct(o.shape, BF16)
    return pl.pallas_call(
        reduce_kernel,
        out_shape=(large, large, small, small),
        in_specs=[hbm, hbm, hbm],
        out_specs=(vmem, vmem, vmem, vmem),
        scratch_shapes=[
            pltpu.VMEM((16, PER, DH), BF16),
            pltpu.VMEM((16, PER, DH), BF16),
            pltpu.VMEM((3, 2, HALF, DH), BF16),
            pltpu.VMEM((3, 2, PER, DH), BF16),
            pltpu.VMEM((NZ + 1, PER, DH), BF16),
            dma((16,)),
            dma((43,)),
            dma((16,)),
            dma((3, 2)),
            dma((3, 2, 2)),
            dma((NZ + 1,)),
            dma((2, 2)),
            dma((2, 2)),
        ],
        compiler_params=pltpu.CompilerParams(
            collective_id=2, has_side_effects=True, vmem_limit_bytes=67043328
        ),
    )(part, o, dq)


def deliver_kernel(*refs):
    n = (len(refs) - 2) // 3
    sources, targets, held, in_sem, out_sem = refs[:n], refs[n : 2 * n], refs[2 * n : 3 * n], refs[-2], refs[-1]
    step = HALF
    parts = [(i, r) for i in range(n) for r in range(0, sources[i].shape[0], step)]

    def copy(m, a, b, sem):
        i, r = parts[m]
        return pltpu.make_async_copy(a[i].at[pl.ds(r, step), :], b[i].at[pl.ds(r, step), :], sem.at[m])

    for m in range(len(parts)):
        copy(m, sources, held, in_sem).start()
    for m in range(len(parts)):
        copy(m, sources, held, in_sem).wait()
        copy(m, held, targets, out_sem).start()
    for m in range(len(parts)):
        copy(m, held, targets, out_sem).wait()


def deliver(*arrays):
    n = len(arrays)
    parts = sum(a.shape[0] // HALF for a in arrays)
    hbm = pl.BlockSpec(memory_space=pl.ANY)
    return pl.pallas_call(
        deliver_kernel,
        out_shape=tuple(jax.ShapeDtypeStruct(a.shape, a.dtype) for a in arrays),
        in_specs=[hbm] * n,
        out_specs=(hbm,) * n,
        scratch_shapes=[pltpu.VMEM(a.shape, a.dtype) for a in arrays]
        + [pltpu.SemaphoreType.DMA((parts,)), pltpu.SemaphoreType.DMA((parts,))],
        compiler_params=pltpu.CompilerParams(vmem_limit_bytes=67043328),
    )(*arrays)


def shards(queries, keys, values, grad_out, doc_lengths, block_plan):
    tok = queries.shape[0]
    n_ctx = lax.axis_size("ctx")
    rank = lax.axis_index("ctx").astype(jnp.int32).reshape(1)
    q = queries.reshape(tok * GROUP, DH)
    g = grad_out.reshape(tok * GROUP, DH)
    kv, q_lent, g_lent = gather(keys.reshape(tok, DH), values.reshape(tok, DH), q, g, n_ctx)
    out, dq, part = attend(rank, doc_lengths, block_plan, q, g, q_lent, g_lent, kv)
    out, dq, dk, dv = deliver(*reduce(part, out, dq))
    return (
        out.reshape(tok, GROUP, DH),
        dq.reshape(tok, GROUP, DH),
        dk.reshape(tok, 1, DH),
        dv.reshape(tok, 1, DH),
    )


def solution(mesh):
    split = P("ctx", "head", None)
    return jax.shard_map(
        shards,
        mesh=mesh,
        in_specs=(split, split, split, split, P(), P()),
        out_specs=(split, split, split, split),
        check_vma=False,
    )
```

```python
import math

import jax
import jax.numpy as jnp
from jax import lax
from jax.experimental import pallas as pl
from jax.experimental.pallas import tpu as pltpu
from jax.sharding import PartitionSpec as P

DH = 128
GROUP = 4
BLK = 512
DOC_MOST = 4096
NDOC = 8
QT = 256
ROWS = QT * GROUP
KT = 256
UNROLL = 4
MAXT = (DOC_MOST + QT) // KT
TILES = 4
PER = 1024
NEG = -1e30
SCALE = 1.0 / math.sqrt(DH)
CONST = SCALE * math.log2(math.e)
F32 = jnp.float32
BF16 = jnp.bfloat16


def mm(a, b):
    return jnp.dot(a, b, preferred_element_type=F32)


def attend_kernel(
    rank_ref, len_ref, plan_ref, q_own, g_own, q_lent, g_lent, kv_ref, o_ref, dq_ref, dkv_ref,
    inv_ref, end_ref, first_ref, last_ref, s_ref, p_ref, kv_buf, acc_kv, zeros, q_ref, g_ref,
    qt_ref, gt_ref, gs_ref, m_ref, acc_ref, dqt_ref, load_sem, store_sem, zero_sem, q_sem, o_buf, dq_buf, give_sem,
):
    n_blocks = plan_ref.shape[0]
    rank = rank_ref[0]
    core = rank % 2

    def side_of(u):
        return (u % 2 + core) % 2

    def fetch(u):
        if u < 2:
            rows = pl.ds(pl.multiple_of((u * 2 + side_of(u)) * ROWS, ROWS), ROWS)
            pair = (q_own, g_own)
        else:
            rows = pl.ds((u - 2) * ROWS, ROWS)
            pair = (q_lent, g_lent)
        into = pl.ds(u * ROWS, ROWS)
        return [
            pltpu.make_async_copy(source.at[rows, :], target.at[into, :], q_sem.at[u, a])
            for a, (source, target) in enumerate(zip(pair, (q_ref, g_ref)))
        ]

    fetches = [fetch(u) for u in range(TILES)]
    for copies in fetches:
        for copy in copies:
            copy.start()

    def invert(i, c):
        inv_ref[plan_ref[i]] = i
        return c

    lax.fori_loop(0, n_blocks, invert, 0)
    end_ref[0] = 0
    for d in range(NDOC):
        end_ref[d + 1] = end_ref[d] + len_ref[d]

    def start_of(position):
        first = jnp.int32(0)
        for d in range(1, NDOC):
            first = jnp.where(position >= end_ref[d], end_ref[d], first)
        return first

    def pos_of(u):
        holder = jnp.where(u < 2, rank, rank + 1 - 2 * core)
        return plan_ref[holder * 2 + u % 2] * BLK + side_of(u) * QT

    def home(kb, j):
        rb = inv_ref[kb]
        base = (rb // 2) * (2 * PER) + j * PER + (rb % 2) * BLK
        return pl.ds(pl.multiple_of(base, BLK), BLK)

    def part(kt):
        return kt // 2, pl.ds(pl.multiple_of((kt % 2) * KT, KT), KT)

    def load(kt, j):
        return pltpu.make_async_copy(kv_ref.at[home(kt, j), :], kv_buf.at[kt, j], load_sem.at[kt, j])

    def store(kt, j):
        return pltpu.make_async_copy(kv_buf.at[kt, j], dkv_ref.at[home(kt, j), :], store_sem.at[kt, j])

    def blank(kt, j):
        return pltpu.make_async_copy(zeros, dkv_ref.at[home(kt, j), :], zero_sem)

    def over(u, action, mark=None):
        pos0 = pos_of(u)

        def body(kt, c):
            if mark is None:
                action(kt)
            else:
                pl.when(mark[kt] == u)(lambda: action(kt))
            return c

        lax.fori_loop(start_of(pos0) // BLK, pos0 // BLK + 1, body, 0)

    def begin(kt):
        for j in (0, 1):
            load(kt, j).start()

    def clear(kt):
        acc_kv[kt] = jnp.zeros((2, BLK, DH), F32)

    def ready(kt):
        for j in (0, 1):
            load(kt, j).wait()

    def finish(kt):
        kv_buf[kt, 0] = (acc_kv[kt, 0] * SCALE).astype(BF16)
        kv_buf[kt, 1] = acc_kv[kt, 1].astype(BF16)
        for j in (0, 1):
            store(kt, j).start()

    def stored(kt):
        for j in (0, 1):
            store(kt, j).wait()

    def blanks(act):
        def body(kt, c):
            @pl.when(first_ref[kt] == TILES)
            def _():
                for j in (0, 1):
                    act(blank(kt, j))

            return c

        lax.fori_loop(0, n_blocks, body, 0)

    def unmark(kt, c):
        first_ref[kt] = TILES
        last_ref[kt] = TILES
        return c

    lax.fori_loop(0, n_blocks, unmark, 0)
    for u in range(TILES):

        def mark(kt, u=u):
            last_ref[kt] = u

            @pl.when(first_ref[kt] == TILES)
            def _():
                first_ref[kt] = u
                begin(kt)
                clear(kt)

        over(u, mark)
    zeros[...] = jnp.zeros(zeros.shape, BF16)
    blanks(lambda copy: copy.start())

    def give(u, a):
        rows = pl.ds(pl.multiple_of(u * ROWS, ROWS), ROWS)
        source, target = ((o_buf, o_ref), (dq_buf, dq_ref))[a]
        return pltpu.make_async_copy(source.at[rows, :], target.at[rows, :], give_sem.at[u, a])

    def tile(u, c):
        pos0 = pos_of(u)
        rows = pl.ds(pl.multiple_of(u * ROWS, ROWS), ROWS)
        last = pos0 // KT
        first = start_of(pos0) // KT
        count = last - first + 1
        q_pos = pos0 + lax.broadcasted_iota(jnp.int32, (1, ROWS), 1) // GROUP
        q_lo = jnp.zeros((1, ROWS), jnp.int32)
        for d in range(1, NDOC):
            q_lo = jnp.where(q_pos >= end_ref[d], end_ref[d], q_lo)
        for a, (source, target) in enumerate(((q_lent, q_ref), (g_lent, g_ref))):
            pltpu.make_async_copy(source.at[pl.ds(0, ROWS), :], target.at[rows, :], q_sem.at[u, a]).wait()
        over(u, ready, first_ref)
        qt_ref[...] = q_ref[rows, :].T
        m_ref[...] = jnp.full(m_ref.shape, NEG, F32)
        acc_ref[...] = jnp.zeros(acc_ref.shape, F32)
        dqt_ref[...] = jnp.zeros(dqt_ref.shape, F32)

        def here(t):
            return pl.ds(pl.multiple_of(t * KT, KT), KT)

        def each(body, total):
            def run(i, c):
                body(i * UNROLL, UNROLL)
                return c

            lax.fori_loop(0, total // UNROLL, run, 0)
            for n in range(1, UNROLL):
                pl.when(total % UNROLL == n)(lambda n=n: body(total - n, n))

        def scores(t0, n, final=False):
            top = m_ref[...]
            for i in range(n):
                kb, at = part(first + t0 + i)
                s = mm(kv_buf[kb, 0, at, :], qt_ref[...]) * CONST
                k_pos = (first + t0 + i) * KT + lax.broadcasted_iota(jnp.int32, (KT, 1), 0)
                seen = k_pos >= q_lo
                if final:
                    seen = seen & (k_pos <= q_pos)
                s = jnp.where(seen, s, NEG)
                s_ref[here(t0 + i), :] = s
                top = jnp.maximum(top, jnp.max(s.reshape(KT // 8, 8, ROWS), axis=0))
            m_ref[...] = top

        each(scores, last - first)
        scores(last - first, 1, True)
        m_ref[0:1, :] = jnp.max(m_ref[...], axis=0, keepdims=True)

        def outputs(t0, n):
            total = acc_ref[...]
            for i in range(n):
                kb, at = part(first + t0 + i)
                v = kv_buf[kb, 1, at, :]
                vt = jnp.concatenate([v.T, jnp.ones((16, KT), BF16)], axis=0)
                p = jnp.exp2(s_ref[here(t0 + i), :] - m_ref[0:1, :]).astype(BF16)
                p_ref[here(t0 + i), :] = p
                total = total + mm(vt, p)
            acc_ref[...] = total

        each(outputs, count)
        inv_sum = 1.0 / acc_ref[DH : DH + 1, :]
        out_t = (acc_ref[0:DH, :] * inv_sum).astype(BF16)
        o_buf[rows, :] = out_t.T
        give(u, 0).start()
        g_t = (g_ref[rows, :].T.astype(F32) * inv_sum).astype(BF16)
        gt_ref[...] = g_t
        gs_ref[...] = g_t.T
        m_ref[1:2, :] = jnp.sum(out_t.astype(F32) * g_t.astype(F32), axis=0, keepdims=True)

        def grads(t0, n):
            for i in range(n):
                kb, at = part(first + t0 + i)
                k = kv_buf[kb, 0, at, :]
                p = p_ref[here(t0 + i), :]
                acc_kv[kb, 1, at, :] += mm(p, gs_ref[...])
                dp = mm(kv_buf[kb, 1, at, :], gt_ref[...])
                ds = (p.astype(F32) * (dp - m_ref[1:2, :])).astype(BF16)
                acc_kv[kb, 0, at, :] += mm(ds, q_ref[rows, :])
                dqt_ref[...] += mm(k.T, ds)

        each(grads, count)
        dq_buf[rows, :] = (dqt_ref[...] * SCALE).astype(BF16).T
        give(u, 1).start()
        over(u, finish, last_ref)
        return c

    lax.fori_loop(0, TILES, tile, 0)
    blanks(lambda copy: copy.wait())
    for u in range(TILES):
        over(u, stored, last_ref)
        for a in (0, 1):
            give(u, a).wait()


def attend(rank, doc_lengths, block_plan, q, g, q_lent, g_lent, kv):
    n_rows = q.shape[0]
    n_kv = kv.shape[0]
    n_blocks = n_kv // (2 * BLK)
    smem = pl.BlockSpec(memory_space=pltpu.SMEM)
    hbm = pl.BlockSpec(memory_space=pl.ANY)
    dma = pltpu.SemaphoreType.DMA
    return pl.pallas_call(
        attend_kernel,
        out_shape=(
            jax.ShapeDtypeStruct((n_rows, DH), BF16),
            jax.ShapeDtypeStruct((n_rows, DH), BF16),
            jax.ShapeDtypeStruct((n_kv, DH), BF16),
        ),
        in_specs=[smem, smem, smem, hbm, hbm, hbm, hbm, hbm],
        out_specs=(hbm, hbm, hbm),
        scratch_shapes=[
            pltpu.SMEM((block_plan.shape[0],), jnp.int32),
            pltpu.SMEM((NDOC + 1,), jnp.int32),
            pltpu.SMEM((n_blocks,), jnp.int32),
            pltpu.SMEM((n_blocks,), jnp.int32),
            pltpu.VMEM((MAXT * KT, ROWS), F32),
            pltpu.VMEM((MAXT * KT, ROWS), BF16),
            pltpu.VMEM((n_blocks, 2, BLK, DH), BF16),
            pltpu.VMEM((n_blocks, 2, BLK, DH), F32),
            pltpu.VMEM((BLK, DH), BF16),
            pltpu.VMEM((TILES * ROWS, DH), BF16),
            pltpu.VMEM((TILES * ROWS, DH), BF16),
            pltpu.VMEM((DH, ROWS), BF16),
            pltpu.VMEM((DH, ROWS), BF16),
            pltpu.VMEM((ROWS, DH), BF16),
            pltpu.VMEM((8, ROWS), F32),
            pltpu.VMEM((DH + 16, ROWS), F32),
            pltpu.VMEM((DH, ROWS), F32),
            dma((n_blocks, 2)),
            dma((n_blocks, 2)),
            dma,
            dma((TILES, 2)),
            pltpu.VMEM((TILES * ROWS, DH), BF16),
            pltpu.VMEM((TILES * ROWS, DH), BF16),
            dma((TILES, 2)),
        ],
        compiler_params=pltpu.CompilerParams(vmem_limit_bytes=67043328),
    )(rank, doc_lengths, block_plan, q, g, q_lent, g_lent, kv)


MESH = pl.DeviceIdType.MESH
NZ = 4
HALF = PER // 2


def place():
    me = lax.axis_index("ctx")
    core = me % 2
    z = (me // 2) % NZ
    x = me // (2 * NZ)

    def at(dx, dz, dc):
        return (((x + dx) % 2) * NZ + (z + dz) % NZ) * 2 + (core + dc) % 2

    return at, core


def meet(peers):
    barrier = pltpu.get_barrier_semaphore()
    for peer in peers:
        pl.semaphore_signal(barrier, inc=1, device_id={"ctx": peer}, device_id_type=MESH)
    pl.semaphore_wait(barrier, len(peers))


def arrive(ref, sem):
    pltpu.make_async_copy(ref, ref, sem).wait()


class Outbox:
    def __init__(self, sems):
        self.sems = sems
        self.copies = []

    def send(self, source, target_ref, sem, target):
        copy = pltpu.make_async_remote_copy(
            src_ref=source,
            dst_ref=target_ref,
            send_sem=self.sems.at[len(self.copies)],
            recv_sem=sem,
            device_id={"ctx": target},
            device_id_type=MESH,
        )
        copy.start()
        self.copies.append(copy)

    def drain(self):
        for copy in self.copies:
            copy.wait_send()


def gather_kernel(
    k_ref, v_ref, q_ref, g_ref, out_ref, qx_ref, gx_ref, own_sem, send_sem, recv_sem, swap_sem
):
    at, core = place()
    me, other, up, down, twin = at(0, 0, 0), at(1, 0, 0), at(0, 1, 0), at(0, NZ - 1, 0), at(0, 0, 1)
    meet((other, up, down, twin))
    box = Outbox(send_sem)

    def slot(owner, j, h):
        return out_ref.at[pl.ds(pl.multiple_of(owner * (2 * PER) + j * PER + h * HALF, HALF), HALF), :]

    def sem(owner, j, h):
        return recv_sem.at[owner * 4 + j * 2 + h]

    def own(j, h):
        return (k_ref, v_ref)[j].at[pl.ds(h * HALF, HALF), :]

    def push(j, h, targets):
        for target in targets:
            box.send(own(j, h), slot(me, j, h), sem(me, j, h), target)

    push(1, 0, (up, down))
    push(0, 0, (other,))
    push(1, 1, (up, down))
    push(0, 1, (other,))
    push(0, 0, (up, down))
    push(1, 0, (other,))
    push(0, 1, (up, down))
    push(1, 1, (other,))
    for i in (0, 1):
        rows = pl.ds(pl.multiple_of((i * 2 + (i + core + 1) % 2) * PER, PER), PER)
        into = pl.ds(i * PER, PER)
        box.send(q_ref.at[rows, :], qx_ref.at[into, :], swap_sem.at[i], twin)
        box.send(g_ref.at[rows, :], gx_ref.at[into, :], swap_sem.at[2 + i], twin)
    keep = []
    for j in (0, 1):
        for h in (0, 1):
            push(j, h, (twin,))
            keep.append(pltpu.make_async_copy(own(j, h), slot(me, j, h), own_sem.at[j * 2 + h]))
            keep[-1].start()

    def relay(dx, dz, j, h, targets):
        owner = at(dx, dz, 0)
        arrive(slot(owner, j, h), sem(owner, j, h))
        for target in targets:
            box.send(slot(owner, j, h), slot(owner, j, h), sem(owner, j, h), target)

    relay(0, 3, 1, 0, (up, other, twin))
    relay(0, 1, 1, 0, (other, twin))
    relay(1, 0, 0, 0, (up, down, twin))
    relay(0, 3, 1, 1, (other, twin))
    relay(0, 1, 1, 1, (down, other, twin))
    relay(1, 0, 0, 1, (up, down, twin))
    relay(0, 3, 0, 0, (up, twin))
    relay(0, 1, 0, 0, (twin,))
    relay(1, 0, 1, 0, (twin,))
    relay(0, 3, 0, 1, (twin,))
    relay(0, 1, 0, 1, (down, twin))
    relay(1, 0, 1, 1, (twin,))
    relay(0, 2, 1, 0, (other, twin))
    relay(0, 2, 1, 1, (other, twin))
    relay(1, 3, 0, 0, (up, twin))
    relay(1, 1, 0, 0, (twin,))
    relay(1, 3, 0, 1, (twin,))
    relay(1, 1, 0, 1, (down, twin))
    for dz in (3, 1):
        for h in (0, 1):
            relay(1, dz, 1, h, (twin,))
    for h in (0, 1):
        relay(0, 2, 0, h, (twin,))
    for h in (0, 1):
        relay(1, 2, 0, h, (twin,))
    for h in (0, 1):
        relay(1, 2, 1, h, (twin,))
    for dx in (0, 1):
        for dz in range(NZ):
            owner = at(dx, dz, 1)
            for j in (0, 1):
                for h in (0, 1):
                    arrive(slot(owner, j, h), sem(owner, j, h))
    for i in (0, 1):
        into = pl.ds(i * PER, PER)
        arrive(qx_ref.at[into, :], swap_sem.at[i])
        arrive(gx_ref.at[into, :], swap_sem.at[2 + i])
    for copy in keep:
        copy.wait()
    box.drain()


def gather(k, v, q, g, n_ctx):
    hbm = pl.BlockSpec(memory_space=pl.ANY)
    dma = pltpu.SemaphoreType.DMA
    return pl.pallas_call(
        gather_kernel,
        out_shape=(
            jax.ShapeDtypeStruct((n_ctx * 2 * PER, DH), BF16),
            jax.ShapeDtypeStruct((2 * PER, DH), BF16),
            jax.ShapeDtypeStruct((2 * PER, DH), BF16),
        ),
        in_specs=[hbm, hbm, hbm, hbm],
        out_specs=(hbm, hbm, hbm),
        scratch_shapes=[dma((4,)), dma((80,)), dma((4 * n_ctx,)), dma((4,))],
        compiler_params=pltpu.CompilerParams(
            collective_id=1, has_side_effects=True, vmem_limit_bytes=67043328
        ),
    )(k, v, q, g)


ORDER = (
    (1, 1, 2), (0, 1, 2), (1, 1, 1), (0, 1, 1), (0, 1, 3), (1, 1, 3), (0, 0, 2), (1, 1, 0),
    (0, 0, 1), (0, 0, 3), (1, 0, 2), (1, 0, 1), (1, 0, 3), (0, 1, 0), (1, 0, 0), (0, 0, 0),
)


def reduce_kernel(
    part_ref, o_ref, dq_ref, out_ref, gq_ref, dk_ref, dv_ref, mine, sib, rel, zin, xin,
    load_sem, send_sem, sib_sem, rel_sem, zin_sem, xin_sem, swap_sem, keep_sem,
):
    at, core = place()
    other, up, down, twin = at(1, 0, 0), at(0, 1, 0), at(0, NZ - 1, 0), at(0, 0, 1)
    meet((other, up, down, twin))
    box = Outbox(send_sem)

    def rows_of(j, owner):
        return part_ref.at[pl.ds(pl.multiple_of(owner * (2 * PER) + j * PER, PER), PER), :]

    loads = []
    for n, (j, dx, dz) in enumerate(ORDER):
        box.send(rows_of(j, at(dx, dz, 1)), sib.at[n], sib_sem.at[n], twin)
        loads.append(pltpu.make_async_copy(rows_of(j, at(dx, dz, 0)), mine.at[n], load_sem.at[n]))
        loads[n].start()
    keep = []
    for a, (source, target) in enumerate(((o_ref, out_ref), (dq_ref, gq_ref))):
        for i in (0, 1):
            kept = pl.ds(pl.multiple_of((i * 2 + (i + core) % 2) * PER, PER), PER)
            keep.append(
                pltpu.make_async_copy(source.at[pl.ds(i * PER, PER), :], target.at[kept, :], keep_sem.at[a, i])
            )
            keep[-1].start()
            box.send(
                source.at[pl.ds((2 + i) * PER, PER), :], target.at[kept, :], swap_sem.at[a, i], twin
            )

    def total(target, others, count):
        step = 256

        def body(i, c):
            rows = pl.ds(pl.multiple_of(i * step, step), step)
            value = others[0][rows, :].astype(F32)
            for ref in others[1:]:
                value = value + ref[rows, :].astype(F32)
            target[rows, :] = value.astype(BF16)
            return c

        lax.fori_loop(0, count // step, body, 0)

    def half(ref, h):
        return ref.at[pl.ds(h * HALF, HALF), :]

    def pair(j, dx, dz):
        n = ORDER.index((j, dx, dz))
        loads[n].wait()
        arrive(sib.at[n], sib_sem.at[n])
        return mine.at[n], sib.at[n]

    def joined(j, dx, dz, extra=()):
        a, b = pair(j, dx, dz)
        total(a, [a, b, *extra], PER)
        return a

    def across(j, dz):
        arrive(xin.at[dz], xin_sem.at[dz])
        return xin.at[dz]

    def far(cat, piece):
        box.send(half(piece, 0), rel.at[cat, 0], rel_sem.at[cat, 0], up)
        box.send(half(piece, 1), rel.at[cat, 1], rel_sem.at[cat, 1], down)

    def zsend(cat, side, h, piece):
        box.send(half(piece, h), half(zin.at[cat, side], h), zin_sem.at[cat, side, h], (up, down)[side])

    def pass_on(cat, above, below):
        arrive(rel.at[cat, 0], rel_sem.at[cat, 0])
        total(half(above, 0), [half(above, 0), rel.at[cat, 0]], HALF)
        zsend(cat, 0, 0, above)
        arrive(rel.at[cat, 1], rel_sem.at[cat, 1])
        total(half(below, 1), [half(below, 1), rel.at[cat, 1]], HALF)
        zsend(cat, 1, 1, below)

    def sides(cat):
        for h in (1, 0):
            for side in (0, 1):
                arrive(half(zin.at[cat, side], h), zin_sem.at[cat, side, h])
        return [zin.at[cat, 0], zin.at[cat, 1]]

    def cross(dz):
        box.send(joined(1, 1, dz), xin.at[dz], xin_sem.at[dz], other)

    cross(2)
    far(0, joined(0, 1, 2))
    cross(1)
    above = joined(0, 1, 1)
    zsend(0, 0, 1, above)
    below = joined(0, 1, 3)
    zsend(0, 1, 0, below)
    cross(3)
    pass_on(0, above, below)
    far(1, joined(0, 0, 2))
    cross(0)
    above = joined(0, 0, 1)
    zsend(1, 0, 1, above)
    below = joined(0, 0, 3)
    zsend(1, 1, 0, below)
    far(2, joined(1, 0, 2, (across(1, 2),)))
    pass_on(1, above, below)
    above = joined(1, 0, 1, (across(1, 1),))
    zsend(2, 0, 1, above)
    below = joined(1, 0, 3, (across(1, 3),))
    zsend(2, 1, 0, below)
    box.send(joined(0, 1, 0, sides(0)), xin.at[NZ], xin_sem.at[NZ], other)
    pass_on(2, above, below)
    near = pair(1, 0, 0)
    total(dv_ref, [*near, across(1, 0), *sides(2)], PER)
    near = pair(0, 0, 0)
    near = [*near, *sides(1)]
    total(dk_ref, [*near, across(0, NZ)], PER)
    for copy in keep:
        copy.wait()
    for a, target in enumerate((out_ref, gq_ref)):
        for i in (0, 1):
            lent = pl.ds(pl.multiple_of((i * 2 + (i + core + 1) % 2) * PER, PER), PER)
            arrive(target.at[lent, :], swap_sem.at[a, i])
    box.drain()


def reduce(part, o, dq):
    vmem = pl.BlockSpec(memory_space=pltpu.VMEM)
    hbm = pl.BlockSpec(memory_space=pl.ANY)
    dma = pltpu.SemaphoreType.DMA
    small = jax.ShapeDtypeStruct((PER, DH), BF16)
    large = jax.ShapeDtypeStruct(o.shape, BF16)
    return pl.pallas_call(
        reduce_kernel,
        out_shape=(large, large, small, small),
        in_specs=[hbm, hbm, hbm],
        out_specs=(vmem, vmem, vmem, vmem),
        scratch_shapes=[
            pltpu.VMEM((16, PER, DH), BF16),
            pltpu.VMEM((16, PER, DH), BF16),
            pltpu.VMEM((3, 2, HALF, DH), BF16),
            pltpu.VMEM((3, 2, PER, DH), BF16),
            pltpu.VMEM((NZ + 1, PER, DH), BF16),
            dma((16,)),
            dma((43,)),
            dma((16,)),
            dma((3, 2)),
            dma((3, 2, 2)),
            dma((NZ + 1,)),
            dma((2, 2)),
            dma((2, 2)),
        ],
        compiler_params=pltpu.CompilerParams(
            collective_id=2, has_side_effects=True, vmem_limit_bytes=67043328
        ),
    )(part, o, dq)


def deliver_kernel(*refs):
    n = (len(refs) - 2) // 3
    sources, targets, held, in_sem, out_sem = refs[:n], refs[n : 2 * n], refs[2 * n : 3 * n], refs[-2], refs[-1]
    step = HALF
    parts = [(i, r) for i in range(n) for r in range(0, sources[i].shape[0], step)]

    def copy(m, a, b, sem):
        i, r = parts[m]
        return pltpu.make_async_copy(a[i].at[pl.ds(r, step), :], b[i].at[pl.ds(r, step), :], sem.at[m])

    for m in range(len(parts)):
        copy(m, sources, held, in_sem).start()
    for m in range(len(parts)):
        copy(m, sources, held, in_sem).wait()
        copy(m, held, targets, out_sem).start()
    for m in range(len(parts)):
        copy(m, held, targets, out_sem).wait()


def deliver(*arrays):
    n = len(arrays)
    parts = sum(a.shape[0] // HALF for a in arrays)
    hbm = pl.BlockSpec(memory_space=pl.ANY)
    return pl.pallas_call(
        deliver_kernel,
        out_shape=tuple(jax.ShapeDtypeStruct(a.shape, a.dtype) for a in arrays),
        in_specs=[hbm] * n,
        out_specs=(hbm,) * n,
        scratch_shapes=[pltpu.VMEM(a.shape, a.dtype) for a in arrays]
        + [pltpu.SemaphoreType.DMA((parts,)), pltpu.SemaphoreType.DMA((parts,))],
        compiler_params=pltpu.CompilerParams(vmem_limit_bytes=67043328),
    )(*arrays)


def shards(queries, keys, values, grad_out, doc_lengths, block_plan):
    tok = queries.shape[0]
    n_ctx = lax.axis_size("ctx")
    rank = lax.axis_index("ctx").astype(jnp.int32).reshape(1)
    q = queries.reshape(tok * GROUP, DH)
    g = grad_out.reshape(tok * GROUP, DH)
    kv, q_lent, g_lent = gather(keys.reshape(tok, DH), values.reshape(tok, DH), q, g, n_ctx)
    out, dq, part = attend(rank, doc_lengths, block_plan, q, g, q_lent, g_lent, kv)
    out, dq, dk, dv = deliver(*reduce(part, out, dq))
    return (
        out.reshape(tok, GROUP, DH),
        dq.reshape(tok, GROUP, DH),
        dk.reshape(tok, 1, DH),
        dv.reshape(tok, 1, DH),
    )


def solution(mesh):
    split = P("ctx", "head", None)
    return jax.shard_map(
        shards,
        mesh=mesh,
        in_specs=(split, split, split, split, P(), P()),
        out_specs=(split, split, split, split),
        check_vma=False,
    )
```
